32 devices in a mesh: users: 8 (over z, y), seq: 4 (over x, core).
Axes of the slice: x: 2, y: 2, z: 4, core: 2. Of those that a mesh axis runs over, the one named last changes fastest.
Arguments:
- raw_events: bfloat16 [4, 3072, 512], P('seq', 'users'), may hold values from -6 to 6
- target_user: int32 [4, 3072], P('seq', 'users'), may hold values from 0 to 7, as said below
- target_place: int32 [4, 3072], P('seq', 'users'), may hold values from 0 to 1023, as said below
- send_counts: int32 [4, 8, 8], P('seq', 'users'), may hold values from 0 to 48, as said below
- lengths: int32 [8], P('users'), may hold values from 512 to 1024, as said below
- cotangent: bfloat16 [8, 1024, 512], P('users', 'seq'), may hold values from -0.06591797 to 0.06591797
- encoder_in: bfloat16 [512, 512], replicated, may hold values from -0.25 to 0.25
- encoder_out: bfloat16 [512, 512], replicated, may hold values from -0.25 to 0.25
- proj_weight: bfloat16 [512, 1024], replicated, may hold values from -0.25 to 0.25
- proj_bias: float32 [1024], replicated, may hold values from -3 to 3
- out_weight: bfloat16 [256, 512], replicated, may hold values from -0.375 to 0.375
- out_bias: float32 [512], replicated, may hold values from -3 to 3
Outputs:
- layer_out: bfloat16 [8, 1024, 512], P('users', 'seq')
- grad_proj_weight: bfloat16 [512, 1024], replicated
- grad_proj_bias: float32 [1024], replicated
- grad_out_weight: bfloat16 [256, 512], replicated
- grad_out_bias: float32 [512], replicated
The draws below stay inside these ranges and needn't reach their ends.
Inputs may be any that keep to these rules, and one draw needn't show every extreme that they name: `target_user`: within one ingestion shard the event rows come first, grouped by user in increasing order; the rows after the shard's total of send_counts carry no event. An event of block b has a position in b * 256 to (b + 1) * 256 - 1. The events of a user are exactly its positions 0 to its length - 1, each once. `target_place`: see target_user. send_counts[b, i, u] rows of shard i in block b go to user u; at most 48, and exactly 48 for some shard and user. The counts of a user in block b sum to min(max(length - b * 256, 0), 256). `lengths`: some user has length exactly 1024.
All inputs are finite; a program needn't handle non-finite values.
Results may differ from the reference program's by a relative error of at most 0.0084.
The reference program's roundings to bfloat16 on the way count: a program that leaves them out, or rounds other values in their place, can miss the bound.
Values may be sent and summed in bfloat16 or wider, within the bound.
A program may use at most 64 MiB of HBM per device.

```python
import jax
import jax.numpy as jnp
from jax import lax

D = 512
HEADS = 4
HEAD = 64
F_IN = 512
LS = 256
A = 256
USERS = 8
BLOCKS = 4
L = 1024
CAP = 48
SLOTS = 384
INGEST = 3072
EVENTS = 8192


def event_plan(key):
    lengths = jax.random.randint(jax.random.fold_in(key, 11), (USERS,), L // 2, L + 1, dtype=jnp.int32)
    longest = jax.random.randint(jax.random.fold_in(key, 12), (), 0, USERS, dtype=jnp.int32)
    lengths = lengths.at[longest].set(L)
    block_ids = jnp.arange(BLOCKS, dtype=jnp.int32)
    live_count = jnp.clip(lengths[None, :] - block_ids[:, None] * LS, 0, LS)
    ticket = jnp.arange(SLOTS, dtype=jnp.int32)
    noise = jax.random.randint(jax.random.fold_in(key, 13), (BLOCKS, USERS, SLOTS), 0, 2 ** 19, dtype=jnp.int32)
    chosen = jax.random.randint(jax.random.fold_in(key, 14), (BLOCKS, USERS), 0, USERS, dtype=jnp.int32)
    ranking = noise * SLOTS + ticket[None, None, :]
    ranking = jnp.where((ticket // CAP)[None, None, :] == chosen[:, :, None], ticket[None, None, :] - SLOTS, ranking)
    order = jnp.argsort(ranking, axis=-1)[:, :, :LS].astype(jnp.int32)
    source = order // CAP
    place = jnp.arange(LS, dtype=jnp.int32)
    alive = place[None, None, :] < live_count[:, :, None]
    block_idx = jnp.broadcast_to(block_ids[:, None, None], (BLOCKS, USERS, LS))
    user_idx = jnp.broadcast_to(jnp.arange(USERS, dtype=jnp.int32)[None, :, None], (BLOCKS, USERS, LS))
    counts = jnp.zeros((BLOCKS, USERS, USERS), jnp.int32).at[block_idx, source, user_idx].add(alive.astype(jnp.int32))
    offsets = jnp.cumsum(counts, axis=2) - counts
    per_user = jnp.transpose(counts, (0, 2, 1))
    before = jnp.cumsum(per_user, axis=2) - per_user
    sort_key = jnp.where(alive, source * LS + place[None, None, :], USERS * LS + place[None, None, :])
    inverse = jnp.argsort(jnp.argsort(sort_key, axis=-1), axis=-1).astype(jnp.int32)
    rank = inverse - jnp.take_along_axis(before, source, axis=2)
    row = offsets[block_idx, source, user_idx] + rank
    flat_index = jnp.where(alive, source * SLOTS + row, USERS * SLOTS)
    filler_user = jax.random.randint(jax.random.fold_in(key, 15), (BLOCKS, INGEST), 0, USERS, dtype=jnp.int32)
    filler_place = jax.random.randint(jax.random.fold_in(key, 16), (BLOCKS, INGEST), 0, LS, dtype=jnp.int32)
    filler_place = filler_place + block_ids[:, None] * LS
    target_user = filler_user.at[block_idx, flat_index].set(user_idx, mode='drop')
    target_place = filler_place.at[block_idx, flat_index].set(block_idx * LS + place[None, None, :], mode='drop')
    return (lengths, counts, target_user, target_place)


def draw_target_user(key, part):
    return event_plan(key)[2]


def draw_target_place(key, part):
    return event_plan(key)[3]


def draw_send_counts(key, part):
    return event_plan(key)[1]


def draw_lengths(key, part):
    return event_plan(key)[0]


def strengthened(values, key, source, target, blocks, factor):
    def block_of(axis_at):
        return (jnp.arange(values.shape[axis_at]) // (values.shape[axis_at] // blocks)).reshape((-1,) + (1,) * (values.ndim - 1 - axis_at))

    one_side = jax.random.permutation(key, blocks)[block_of(target)]
    other_side = (block_of(target) + blocks // 2) % blocks
    return jnp.where((block_of(source) == one_side) | (block_of(source) == other_side), factor * values, values)


def block_scale(key, shape, pieces, smallest, top_value):
    factor_of, own = 1.0, jax.random.fold_in(key, 6)
    for dim, parts in pieces:
        heights = jnp.exp(jax.random.uniform(jax.random.fold_in(own, dim), (parts,), jnp.float32, smallest / len(pieces), top_value / len(pieces)))
        factor_of = factor_of * jnp.repeat(heights, shape[dim] // parts).reshape([-1 if axis == dim else 1 for axis in range(len(shape))])
    return factor_of


def scatter_about(rng, dims, scale, reach, shards=(), kind=jnp.bfloat16):
    factor_of = block_scale(rng, dims, shards, -0.22, 0.18) if shards else 1.0
    drawn = jax.random.normal(rng, dims, jnp.float32) * scale * factor_of
    return jnp.minimum(jnp.maximum(drawn, -reach), reach).astype(kind)


def bell_draw_with(rng, dims, spread, most, shards, heavy, kind=jnp.bfloat16):
    drawn = spread * jax.random.normal(rng, dims, jnp.float32)
    if shards:
        drawn = drawn * block_scale(rng, dims, shards, -0.22, 0.18)
    return jnp.clip(strengthened(drawn, jax.random.fold_in(rng, 3), *heavy), -most, most).astype(kind)


def setup_inputs(seed: int = 0) -> dict:
    arg_keys = jax.random.split(jax.random.key(seed), 13)
    raw_events = scatter_about(arg_keys[0], (BLOCKS, INGEST, F_IN), 1.0, 6.0, ((0, 4), (1, 8)))
    target_user = draw_target_user(jax.random.fold_in(arg_keys[12], 71), 0)
    target_place = draw_target_place(jax.random.fold_in(arg_keys[12], 71), 0)
    send_counts = draw_send_counts(jax.random.fold_in(arg_keys[12], 71), 0)
    lengths = draw_lengths(jax.random.fold_in(arg_keys[12], 71), 0)
    cotangent = bell_draw_with(arg_keys[5], (USERS, L, D), (EVENTS ** -0.5), 0.06591797, ((0, 8), (1, 4)), (0, 2, 8, 2.0))
    encoder_in = scatter_about(arg_keys[6], (F_IN, D), F_IN ** -0.5, 0.25)
    encoder_out = scatter_about(arg_keys[7], (D, D), D ** -0.5, 0.25)
    proj_weight = scatter_about(arg_keys[8], (D, 4 * A), D ** -0.5, 0.25)
    proj_bias = scatter_about(arg_keys[9], (4 * A,), 0.5, 3.0, (), jnp.float32)
    out_weight = scatter_about(arg_keys[10], (A, D), A ** -0.5, 0.375)
    out_bias = scatter_about(arg_keys[11], (D,), 0.5, 3.0, (), jnp.float32)
    return dict(raw_events=raw_events, target_user=target_user, target_place=target_place, send_counts=send_counts, lengths=lengths, cotangent=cotangent, encoder_in=encoder_in, encoder_out=encoder_out, proj_weight=proj_weight, proj_bias=proj_bias, out_weight=out_weight, out_bias=out_bias)


EPSILON = 1e-05

def layer_norm(values):
    center = values - lax.optimization_barrier(jnp.mean(values, axis=-1, keepdims=True))
    inverse = lax.rsqrt(lax.optimization_barrier(jnp.mean(center * center, axis=-1, keepdims=True)) + EPSILON)
    return (center * inverse, inverse)

def silu_grad(values):
    sigmoid = jax.nn.sigmoid(values)
    return sigmoid * (1.0 + values * (1.0 - sigmoid))

def one_user(sequence, user_cot, length, proj_weight, proj_bias, out_weight, out_bias):
    width = HEADS * HEAD
    score_scale = HEAD ** (-0.5)
    positions = jnp.arange(L, dtype=jnp.int32)
    present = positions < length
    normed = layer_norm(sequence.astype(jnp.float32))[0].astype(jnp.bfloat16)
    projected = jnp.dot(normed, proj_weight, preferred_element_type=jnp.float32) + proj_bias
    gates = jax.nn.silu(projected).astype(jnp.bfloat16)
    gate_u = gates[:, :width].astype(jnp.float32)
    value_heads = gates[:, width:2 * width].reshape(L, HEADS, HEAD).astype(jnp.float32)
    query_heads = gates[:, 2 * width:3 * width].reshape(L, HEADS, HEAD).astype(jnp.float32)
    key_heads = gates[:, 3 * width:].reshape(L, HEADS, HEAD).astype(jnp.float32)
    scores = jnp.einsum('qhd,khd->hqk', query_heads, key_heads) * score_scale
    allowed = (positions[None, :] <= positions[:, None]) & (positions[None, :] < length)
    weights = jnp.where(allowed, jax.nn.silu(scores), 0.0).astype(jnp.bfloat16)
    weights_wide = weights.astype(jnp.float32)
    attended = jnp.einsum('hqk,khd->qhd', weights_wide, value_heads).reshape(L, width)
    onorm, inverse = layer_norm(attended)
    mixed = (onorm * gate_u).astype(jnp.bfloat16)
    result = jnp.dot(mixed, out_weight, preferred_element_type=jnp.float32) + out_bias + sequence.astype(jnp.float32)
    layer_out = jnp.where(present[:, None], result, 0.0).astype(jnp.bfloat16)
    d_out = jnp.where(present[:, None], user_cot, jnp.zeros_like(user_cot))
    grad_ob = lax.optimization_barrier(jnp.sum(d_out.astype(jnp.float32), axis=0))
    grad_ow = jnp.dot(mixed.T, d_out, preferred_element_type=jnp.float32)
    d_mixed = jnp.dot(d_out, out_weight.T, preferred_element_type=jnp.float32)
    d_gate_u = d_mixed * onorm
    d_onorm = d_mixed * gate_u
    d_att = (d_onorm - lax.optimization_barrier(jnp.mean(d_onorm, axis=-1, keepdims=True)) - onorm * lax.optimization_barrier(jnp.mean(d_onorm * onorm, axis=-1, keepdims=True))) * inverse
    d_att = d_att.astype(jnp.bfloat16)
    d_heads = d_att.reshape(L, HEADS, HEAD).astype(jnp.float32)
    d_weights = jnp.einsum('qhd,khd->hqk', d_heads, value_heads)
    d_values = jnp.einsum('hqk,qhd->khd', weights_wide, d_heads).reshape(L, width)
    d_scores = jnp.where(allowed, d_weights * silu_grad(scores), 0.0).astype(jnp.bfloat16).astype(jnp.float32)
    d_queries = score_scale * jnp.einsum('hqk,khd->qhd', d_scores, key_heads).reshape(L, width)
    d_keys = score_scale * jnp.einsum('hqk,qhd->khd', d_scores, query_heads).reshape(L, width)
    d_proj = jnp.concatenate([d_gate_u, d_values, d_queries, d_keys], axis=1) * silu_grad(projected)
    d_proj = d_proj.astype(jnp.bfloat16)
    grad_pb = lax.optimization_barrier(jnp.sum(d_proj.astype(jnp.float32), axis=0))
    grad_pw = jnp.dot(normed.T, d_proj, preferred_element_type=jnp.float32)
    return (layer_out, grad_pw, grad_pb, grad_ow, grad_ob)

def reference(raw_events, target_user, target_place, send_counts, lengths, cotangent, encoder_in, encoder_out, proj_weight, proj_bias, out_weight, out_bias):
    flat_raw = raw_events.reshape(BLOCKS * INGEST, F_IN)
    enc_hidden = jax.nn.silu(jnp.dot(flat_raw, encoder_in, preferred_element_type=jnp.float32)).astype(jnp.bfloat16)
    encoded = jnp.dot(enc_hidden, encoder_out, preferred_element_type=jnp.float32).astype(jnp.bfloat16)
    totals = lax.optimization_barrier(jnp.sum(send_counts, axis=2))
    row_ids = jnp.arange(INGEST, dtype=jnp.int32)
    shard_of = row_ids // SLOTS
    valid = (row_ids % SLOTS)[None, :] < totals[:, shard_of]
    flat_index = jnp.where(valid, target_user * L + target_place, USERS * L).astype(jnp.int32).reshape(-1)
    sequences = jnp.zeros((USERS * L, D), jnp.bfloat16).at[flat_index].set(encoded, mode='drop')
    sequences = sequences.reshape(USERS, L, D)
    width = HEADS * HEAD
    initial = (jnp.zeros((D, 4 * width), jnp.float32), jnp.zeros((4 * width,), jnp.float32), jnp.zeros((width, D), jnp.float32), jnp.zeros((D,), jnp.float32))

    def advance(running, inputs):
        sequence, user_cot, length = inputs
        layer_out, grad_pw, grad_pb, grad_ow, grad_ob = one_user(sequence, user_cot, length, proj_weight, proj_bias, out_weight, out_bias)
        running = (running[0] + grad_pw, running[1] + grad_pb, running[2] + grad_ow, running[3] + grad_ob)
        return (running, layer_out)
    running, outputs = lax.scan(advance, initial, (sequences, cotangent, lengths))
    return (outputs, running[0].astype(jnp.bfloat16), running[1], running[2].astype(jnp.bfloat16), running[3])
```

```python
import functools

import jax
import jax.numpy as jnp
from jax import lax
from jax.experimental import pallas as pl
from jax.experimental.pallas import tpu as pltpu
from jax.sharding import PartitionSpec as P

HEAD = 64
EPSILON = 1e-05
LANES = 128
ROWS = 16
F32 = jnp.float32
BF16 = jnp.bfloat16


def sigmoid(values):
    return 0.5 * jnp.tanh(0.5 * values) + 0.5


def silu(values):
    return values * sigmoid(values)


def silu_grad(values):
    gate = sigmoid(values)
    return gate * (1.0 + values * (1.0 - gate))


def layer_norm(values):
    center = values - jnp.mean(values, axis=-1, keepdims=True)
    inverse = lax.rsqrt(jnp.mean(center * center, axis=-1, keepdims=True) + EPSILON)
    return center * inverse, inverse


def dot(a, b, contract=(1, 0)):
    return lax.dot_general(
        a, b, (((contract[0],), (contract[1],)), ((), ())), preferred_element_type=F32
    )


def flip(index, bit):
    return index + bit * (1 - 2 * ((index // bit) % 2))


def flip_all(index, delta):
    bit = 1
    while bit <= delta:
        if delta & bit:
            index = flip(index, bit)
        bit *= 2
    return index


def plan_of(users, seqs, groups):
    near, far = [], []
    bit = 1
    while bit < users:
        near.append(("users", bit))
        bit *= 2
    bit = 2
    while bit < seqs:
        far.append(("seq", bit))
        bit *= 2
    devices = users * seqs // 2
    plans = []
    base = 0
    for chunks, most, across_first in groups:
        each = -(-chunks // devices)
        if across_first:
            turn = (far + near)[:3]
            tail = (far + near)[3:]
        else:
            turn = near[:2]
            tail = near[2:] + far
        streams = []
        for i in range(most):
            share = (each + most - 1 - i) // most
            if share == 0:
                continue
            k = i % len(turn)
            streams.append((base, share * devices, turn[k:] + turn[:k] + tail))
            base += share * devices
        plans.append(streams)
    return plans, len(near) + len(far), base


def groups_of(model, share):
    tile = ROWS * LANES
    return (
        (2 * model * share // tile, 2, False),
        (model * share // tile, 2, False),
        (2 * model * share // tile, 4, True),
    )


def kernel(
    users,
    seqs,
    raw_hbm,
    user_ref,
    place_ref,
    counts_ref,
    length_ref,
    cot_hbm,
    enc_in_hbm,
    enc_out_hbm,
    proj_w_hbm,
    proj_b_ref,
    out_w_hbm,
    out_b_ref,
    layer_ref,
    full,
    bias_ref,
    send_buf,
    rows_sc,
    spot_out,
    spot_in,
    seq_sc,
    norm_sc,
    proj_sc,
    gate_sc,
    v_sc,
    k_sc,
    qb,
    gb,
    w_sc,
    s_sc,
    att,
    dq,
    dk,
    dv,
    d_mix,
    dproj,
    stat_out,
    stat_in,
    mix_own,
    mix_in,
    work,
    landing,
    bias,
    bias_in,
    raw_ref,
    cots,
    enc_in_ref,
    enc_out_ref,
    proj_w_ref,
    out_w_ref,
    a2a_send,
    a2a_recv,
    spot_send,
    spot_recv,
    x_send,
    x_recv,
    xs_send,
    xs_recv,
    n_send,
    n_recv,
    cot_sem,
    stat_sem,
    mix_sem,
    q_send,
    q_recv,
    g_send,
    g_recv,
    rs_send,
    rs_recv,
    ag_send,
    ag_recv,
    core_send,
    core_recv,
    b_send,
    b_recv,
    in_sem,
):
    me_u = lax.axis_index("users")
    me_s = lax.axis_index("seq")
    MESH = pl.DeviceIdType.MESH
    slots, model = raw_ref.shape
    block = layer_ref.shape[0]
    span = 2 * block
    width = out_w_ref.shape[0]
    share = width // 2
    pairs = share // LANES
    cap_pad = send_buf.shape[1]
    halves = seqs // 2
    scale = HEAD ** (-0.5)
    mine = me_s % 2
    half = me_s // 2
    partner = (me_u, flip(me_s, 1))

    def at_half(h):
        return (me_u, h * 2 + mine)

    def remote(source, target, send_sem, recv_sem, device):
        return pltpu.make_async_remote_copy(
            src_ref=source,
            dst_ref=target,
            send_sem=send_sem,
            recv_sem=recv_sem,
            device_id=device,
            device_id_type=MESH,
        )

    barrier = pltpu.get_barrier_semaphore()
    greeted = [(lax.rem(me_u + delta, users), me_s) for delta in range(1, users)]
    greeted += [partner]
    greeted += [at_half(lax.rem(half + delta, halves)) for delta in range(1, halves)]
    for device in greeted:
        pl.semaphore_signal(barrier, inc=1, device_id=device, device_id_type=MESH)

    def own_columns(part):
        return pl.ds(pl.multiple_of(part * width + mine * share, LANES), share)

    parts = (0, 2, 1, 3)
    loads = [
        pltpu.make_async_copy(source, target, in_sem.at[i])
        for i, (source, target) in enumerate(
            [
                (raw_hbm, raw_ref),
                (cot_hbm, cots.at[mine]),
                (out_w_hbm, out_w_ref),
                (enc_in_hbm, enc_in_ref),
                (enc_out_hbm, enc_out_ref),
            ]
            + [
                (
                    proj_w_hbm.at[:, own_columns(part)],
                    proj_w_ref.at[:, i * share : (i + 1) * share],
                )
                for i, part in enumerate(parts)
            ]
        )
    ]
    for load in loads:
        load.start()

    target = user_ref[...]
    lane_row = lax.broadcasted_iota(jnp.int32, (1, slots), 1)
    first = jnp.zeros((1, slots), jnp.int32)
    total = jnp.int32(0)
    for u in range(users):
        first = jnp.where(target == u, total, first)
        total = total + counts_ref[0, u]
    flat = jnp.where(lane_row < total, target * cap_pad + lane_row - first, -1)
    hot = lax.broadcasted_iota(jnp.int32, (users * cap_pad, slots), 0) == flat
    local_place = (place_ref[...] - me_s * block + 1).astype(F32)
    spots = jnp.sum(jnp.where(hot, local_place, 0.0), axis=1, keepdims=True) - 1.0
    diagonal = lax.broadcasted_iota(
        jnp.int32, (users, cap_pad, LANES), 1
    ) == lax.broadcasted_iota(jnp.int32, (users, cap_pad, LANES), 2)
    spot_out[...] = jnp.sum(
        jnp.where(diagonal, spots.reshape(users, cap_pad, 1), 0.0), axis=1, keepdims=True
    )
    loads[0].wait()
    bucket = dot(hot.astype(F32).astype(BF16), raw_ref[...]).astype(BF16)
    send_buf[...] = bucket.reshape(users, cap_pad, model)

    pl.semaphore_wait(barrier, len(greeted))

    order = list(range(users - 1, 0, -1))

    def spot_copy(d):
        peer = flip_all(me_u, d)
        return remote(
            spot_out.at[peer], spot_in.at[half, me_u], spot_send.at[d], spot_recv.at[d], (peer, me_s)
        )

    def row_copy(d):
        peer = flip_all(me_u, d)
        return remote(
            send_buf.at[peer], rows_sc.at[half, me_u], a2a_send.at[d], a2a_recv.at[d], (peer, me_s)
        )

    def relay(h, d, delta):
        source = flip_all(me_u, d)
        held = send_buf.at[source] if d == 0 else rows_sc.at[h, source]
        return remote(
            held,
            rows_sc.at[h, source],
            x_send.at[delta - 1, d],
            x_recv.at[delta - 1, d],
            at_half(h + delta),
        )

    def relay_spots(h, delta):
        return remote(
            spot_in.at[h],
            spot_in.at[h],
            xs_send.at[delta - 1],
            xs_recv.at[delta - 1],
            at_half(h + delta),
        )

    def above(delta):
        return half + delta < halves

    def below(delta):
        return half >= delta

    for d in order:
        spot_copy(d).start()
    for d in order:
        row_copy(d).start()
    for delta in range(1, halves):

        @pl.when(above(delta))
        def _():
            relay(half, 0, delta).start()

    loads[1].wait()
    cot_copy = remote(cots.at[mine], cots.at[mine], cot_sem.at[0], cot_sem.at[1], partner)
    cot_copy.start()
    rows_sc[half, me_u] = send_buf[me_u]
    spot_in[half, me_u] = spot_out[me_u]

    length = length_ref[0]
    rows = lax.broadcasted_iota(jnp.int32, (block, 1), 0)

    def block_rows(index):
        return pl.ds(pl.multiple_of(index * block, block), block)

    own_rows, other_rows = block_rows(mine), block_rows(1 - mine)

    def present_at(index):
        return (half * 2 + index) * block + rows < length

    out_rows = pl.ds(pl.multiple_of(mine * share, LANES), share)
    out_rows_other = pl.ds(pl.multiple_of((1 - mine) * share, LANES), share)
    loads[2].wait()

    def mask_cot(index):
        d_out = jnp.where(
            present_at(index), cots[index], jnp.zeros((block, model), BF16)
        )
        d_mix[block_rows(index), :] = dot(d_out, out_w_ref[out_rows, :], (1, 1))

    mask_cot(mine)
    for load in loads[3:]:
        load.wait()
    bias_row = jnp.concatenate([proj_b_ref[:, own_columns(part)] for part in parts], axis=1)
    att[...] = jnp.zeros_like(att)
    dq[...] = jnp.zeros_like(dq)
    dk[...] = jnp.zeros_like(dk)
    dv[...] = jnp.zeros_like(dv)
    cot_copy.wait_recv()
    mask_cot(1 - mine)

    for d in order:
        spot_copy(d).wait_recv()
    for delta in range(1, halves):

        @pl.when(above(delta))
        def _():
            relay_spots(half, delta).start()

    for d in order:
        row_copy(d).wait_recv()
        for delta in range(1, halves):

            @pl.when(above(delta))
            def _():
                relay(half, d, delta).start()

    def ingest(h):
        arrived = rows_sc[h].reshape(users * cap_pad, model)
        where_to = jnp.sum(jnp.where(diagonal, spot_in[h], 0.0), axis=2, keepdims=True)
        where_to = where_to.reshape(users * cap_pad, 1).astype(jnp.int32)
        placed = (
            lax.broadcasted_iota(jnp.int32, (users * cap_pad, block), 1) == where_to
        ).astype(F32).astype(BF16)
        events = dot(placed, arrived, (0, 0)).astype(BF16)
        hidden = silu(dot(events, enc_in_ref[...])).astype(BF16)
        sequence = dot(hidden, enc_out_ref[...]).astype(BF16)
        norm_sc[h, mine] = layer_norm(sequence.astype(F32))[0].astype(BF16)
        return sequence

    def norm_copy(h):
        own = norm_sc.at[h, mine]
        return remote(own, own, n_send.at[h], n_recv.at[h], partner)

    seq_sc[...] = ingest(half)
    norm_copy(half).start()

    def project(index):
        at = block_rows(index)
        projected = dot(norm_sc[half, index], proj_w_ref[...]) + bias_row
        proj_sc[at, :] = projected
        gates = silu(projected).astype(BF16)
        gate_sc[at, :] = gates[:, :share]
        qb[half, at, :] = gates[:, share : 2 * share]
        v_sc[half, at, :] = gates[:, 2 * share : 3 * share]
        k_sc[half, at, :] = gates[:, 3 * share :]

    def project_low(h, index):
        at = block_rows(index)
        gates = silu(
            dot(norm_sc[h, index], proj_w_ref[:, 2 * share :]) + bias_row[:, 2 * share :]
        ).astype(BF16)
        v_sc[h, at, :] = gates[:, :share]
        k_sc[h, at, :] = gates[:, share:]

    project(mine)

    for delta in range(1, halves):

        @pl.when(below(delta))
        def _():
            h = half - delta
            relay_spots(h, delta).wait_recv()
            for d in [0] + order:
                relay(h, d, delta).wait_recv()
            ingest(h)
            norm_copy(h).start()
            project_low(h, mine)

    norm_copy(half).wait_recv()
    project(1 - mine)

    def q_copy(delta):
        return remote(
            qb.at[half], qb.at[half], q_send.at[delta - 1], q_recv.at[delta - 1], at_half(half - delta)
        )

    for delta in range(1, halves):

        @pl.when(below(delta))
        def _():
            q_copy(delta).start()

    def half_of(values, hh):
        zero = jnp.zeros_like(values)
        low = lax.broadcasted_iota(jnp.int32, values.shape, 1) < HEAD
        return jnp.where(low, values, zero) if hh == 0 else jnp.where(low, zero, values)

    def lanes(p):
        return slice(p * LANES, (p + 1) * LANES)

    def merge(low, high):
        keep = lax.broadcasted_iota(jnp.int32, low.shape, 1) < HEAD
        return jnp.where(keep, low, high)

    def scores_of(slot, q_half, k_half, qi, keys_to):
        qr = slice(qi * block, (qi + 1) * block)
        kr = slice(0, keys_to * block)
        bound = jnp.minimum((q_half * 2 + qi) * block + rows, length - 1) - k_half * span
        allowed = lax.broadcasted_iota(jnp.int32, (block, keys_to * block), 1) <= bound
        for p in range(pairs):
            queries = qb[q_half, qr, lanes(p)]
            keys = k_sc[k_half, kr, lanes(p)]
            for hh in range(2):
                score = dot(half_of(queries, hh), keys, (1, 1)) * scale
                gate = sigmoid(score)
                plain = score * gate
                w_sc[slot, 2 * p + hh, qr, kr] = jnp.where(allowed, plain, 0.0).astype(BF16)
                s_sc[slot, 2 * p + hh, qr, kr] = jnp.where(
                    allowed, gate + plain * (1.0 - gate), 0.0
                )

    def attend(slot, k_half, qi, keys_to):
        qr = slice(qi * block, (qi + 1) * block)
        kr = slice(0, keys_to * block)
        for p in range(pairs):
            values = v_sc[k_half, kr, lanes(p)]
            att[qr, lanes(p)] = att[qr, lanes(p)] + merge(
                dot(w_sc[slot, 2 * p, qr, kr], values), dot(w_sc[slot, 2 * p + 1, qr, kr], values)
            )

    for qi in range(2):
        scores_of(half, half, half, qi, qi + 1)
        attend(half, half, qi, qi + 1)

    for delta in range(1, halves):

        @pl.when(below(delta))
        def _():
            h = half - delta
            norm_copy(h).wait_recv()
            project_low(h, 1 - mine)
            for qi in range(2):
                scores_of(h, half, h, qi, 2)
                attend(h, h, qi, 2)

    attended = att[...]
    gate_u = gate_sc[...].astype(F32)
    d_mixed = d_mix[...]
    d_onorm = d_mixed * gate_u
    own_mean = jnp.mean(attended, axis=-1, keepdims=True)
    center = attended - own_mean
    facts = (
        own_mean,
        jnp.sum(center * center, axis=-1, keepdims=True),
        jnp.sum(d_onorm, axis=-1, keepdims=True),
        jnp.sum(d_onorm * center, axis=-1, keepdims=True),
    )
    tall = span // LANES
    square = lax.broadcasted_iota(jnp.int32, (tall, LANES, LANES), 1) == lax.broadcasted_iota(
        jnp.int32, (tall, LANES, LANES), 2
    )
    for i, fact in enumerate(facts):
        stat_out[i] = jnp.sum(
            jnp.where(square, fact.reshape(tall, LANES, 1), 0.0), axis=1, keepdims=True
        )
    stat_copy = remote(stat_out, stat_in, stat_sem.at[0], stat_sem.at[1], partner)
    stat_copy.start()

    stat_copy.wait_recv()
    theirs = [
        jnp.sum(jnp.where(square, stat_in[i], 0.0), axis=2, keepdims=True).reshape(span, 1)
        for i in range(len(facts))
    ]
    mean = 0.5 * (own_mean + theirs[0])
    gap = own_mean - theirs[0]
    variance = (facts[1] + theirs[1] + gap * gap * (0.5 * share)) / width
    inverse = lax.rsqrt(variance + EPSILON)
    mean_d = (facts[2] + theirs[2]) / width
    mean_do = (
        (facts[3] + theirs[3] + (own_mean - mean) * facts[2] + (theirs[0] - mean) * theirs[2])
        * inverse
        / width
    )
    onorm = (attended - mean) * inverse
    d_att = ((d_onorm - mean_d - onorm * mean_do) * inverse).astype(BF16)
    gb[half] = d_att

    def g_copy(delta, qi):
        piece = gb.at[half, qi * block : (qi + 1) * block]
        return remote(
            piece, piece, g_send.at[delta - 1, qi], g_recv.at[delta - 1, qi], at_half(half - delta)
        )

    for delta in range(1, halves):

        @pl.when(below(delta))
        def _():
            for qi in range(2):
                g_copy(delta, qi).start()

    mixed = (onorm * gate_u).astype(BF16)
    mix_own[...] = mixed
    mix_copy = remote(mix_own.at[other_rows], mix_in, mix_sem.at[0], mix_sem.at[1], partner)
    mix_copy.start()
    dproj[:, :share] = (d_mixed * onorm * silu_grad(proj_sc[:, :share])).astype(BF16)
    positions = lax.broadcasted_iota(jnp.int32, (span, 1), 0)
    present = half * span + positions < length
    d_out = jnp.where(present, cots[...].reshape(span, model), jnp.zeros((span, model), BF16))
    normed = norm_sc[half].reshape(span, model)
    column = jnp.sum(d_out.astype(F32), axis=0, keepdims=True)
    bias[0] = jnp.zeros_like(bias[0])
    bias[0, 1:2, : model // 2] = jnp.where(
        mine == 0, column[:, : model // 2], column[:, model // 2 :]
    )
    (early, middle, late), stages, total_chunks = plan_of(users, seqs, groups_of(model, share))
    middle_base, late_base = middle[0][0], late[0][0]

    def store_tiles(base, values):
        height = values.shape[0] // ROWS
        for tile in range(values.shape[1] // LANES):
            work[base + tile * height : base + (tile + 1) * height] = values[
                :, tile * LANES : (tile + 1) * LANES
            ].reshape(height, ROWS, LANES)
        return base + values.shape[0] * values.shape[1] // (ROWS * LANES)

    def clear(base, stop):
        if base < stop:
            work[base:stop] = jnp.zeros((stop - base, ROWS, LANES), BF16)

    filled = store_tiles(0, dot(mixed, d_out, (0, 0)).astype(BF16))
    filled = store_tiles(filled, dot(normed, dproj[:, :share], (0, 0)).astype(BF16))
    clear(filled, middle_base)

    def place_of(axis, bit):
        own = me_s if axis == "seq" else me_u
        peer = flip(own, bit)
        device = (me_u, peer) if axis == "seq" else (peer, me_s)
        return (own // bit) % 2, device

    all_streams = early + middle + late
    starts = [[base] for base, _, _ in all_streams]
    landings = []
    landing_at = 0
    for base, size, _ in all_streams:
        offsets = []
        for stage in range(stages):
            offsets.append(landing_at)
            landing_at += size >> (stage + 1)
        landings.append(offsets)
    early_ids = list(range(len(early)))
    middle_ids = list(range(len(early), len(early) + len(middle)))
    late_ids = list(range(len(early) + len(middle), len(all_streams)))

    def reduce_copy(i, stage):
        base, size, bit_order = all_streams[i]
        side, device = place_of(*bit_order[stage])
        part = size >> (stage + 1)
        start = starts[i][stage]
        return (
            remote(
                work.at[pl.ds(start + (1 - side) * part, part)],
                landing.at[pl.ds(landings[i][stage], part)],
                rs_send.at[i, stage],
                rs_recv.at[i, stage],
                device,
            ),
            start + side * part,
            part,
        )

    def gather_copy(i, stage):
        base, size, bit_order = all_streams[i]
        _, device = place_of(*bit_order[stage])
        own = full.at[mine, pl.ds(starts[i][stage + 1], size >> (stage + 1))]
        return remote(own, own, ag_send.at[i, stage], ag_recv.at[i, stage], device)

    def core_copy(i, second):
        base, size, bit_order = all_streams[i]
        side, _ = place_of(*bit_order[0])
        part = size >> 1
        start = base + (1 - side) * part if second else base + side * part
        own = full.at[mine, pl.ds(start, part)]
        return remote(own, own, core_send.at[i, second], core_recv.at[i, second], partner)

    def reduce_start(ids):
        for i in ids:
            reduce_copy(i, 0)[0].start()

    def reduce_step(ids, stage):
        for i in ids:
            copy, keep, part = reduce_copy(i, stage)
            copy.wait()
            at = landings[i][stage]
            summed = (
                work[pl.ds(keep, part)].astype(F32) + landing[at : at + part].astype(F32)
            ).astype(BF16)
            starts[i].append(keep)
            if stage + 1 < stages:
                work[pl.ds(keep, part)] = summed
                reduce_copy(i, stage + 1)[0].start()
            else:
                full[mine, pl.ds(keep, part)] = summed
                gather_copy(i, stage).start()
                if stage == 0:
                    core_copy(i, 0).start()

    def gather_step(ids, stage):
        for i in ids:
            gather_copy(i, stage).wait()
            if stage > 0:
                gather_copy(i, stage - 1).start()
                if stage == 1:
                    core_copy(i, 0).start()
            else:
                core_copy(i, 1).start()

    def core_finish(ids):
        for i in ids:
            core_copy(i, 0).wait()
            core_copy(i, 1).wait()

    def advance(ids, turn):
        if turn < stages:
            reduce_step(ids, turn)
        elif turn < 2 * stages:
            gather_step(ids, 2 * stages - 1 - turn)
        elif turn == 2 * stages:
            core_finish(ids)

    reduce_start(early_ids)

    for delta in range(1, halves):

        @pl.when(above(delta))
        def _():
            h = half + delta
            remote(
                qb.at[h], qb.at[h], q_send.at[delta - 1], q_recv.at[delta - 1], at_half(half)
            ).wait_recv()
            for qi in range(2):
                scores_of(h, h, half, qi, 2)

    def backward(slot, q_half, k_half, qi, keys_to, query_side, key_side):
        qr = slice(qi * block, (qi + 1) * block)
        kr = slice(0, keys_to * block)
        for p in range(pairs):
            at = lanes(p)
            grads = gb[q_half, qr, at]
            values = v_sc[k_half, kr, at]
            d_scores = []
            for hh in range(2):
                d_weight = dot(half_of(grads, hh), values, (1, 1))
                d_scores.append((d_weight * s_sc[slot, 2 * p + hh, qr, kr]).astype(BF16))
            if query_side:
                keys = k_sc[k_half, kr, at]
                dq[qr, at] = dq[qr, at] + merge(dot(d_scores[0], keys), dot(d_scores[1], keys))
            if key_side:
                queries = qb[q_half, qr, at]
                dk[kr, at] = dk[kr, at] + merge(
                    dot(d_scores[0], queries, (0, 0)), dot(d_scores[1], queries, (0, 0))
                )
                dv[kr, at] = dv[kr, at] + merge(
                    dot(w_sc[slot, 2 * p, qr, kr], grads, (0, 0)),
                    dot(w_sc[slot, 2 * p + 1, qr, kr], grads, (0, 0)),
                )

    for qi in range(2):
        backward(half, half, half, qi, qi + 1, True, True)

    for delta in range(1, halves):

        @pl.when(below(delta))
        def _():
            h = half - delta
            for qi in range(2):
                backward(h, half, h, qi, 2, True, False)

    def finish_part(index, buf, factor):
        at = slice(index * share, (index + 1) * share)
        dproj[:, at] = (buf[...] * factor * silu_grad(proj_sc[:, at])).astype(BF16)

    finish_part(1, dq, scale)
    filled = store_tiles(
        middle_base, dot(normed, dproj[:, share : 2 * share], (0, 0)).astype(BF16)
    )
    clear(filled, late_base)
    reduce_start(middle_ids)

    advance(early_ids, 0)
    advance(early_ids, 1)

    for delta in range(1, halves):

        @pl.when(above(delta))
        def _():
            h = half + delta
            for qi in range(2):
                piece = gb.at[h, qi * block : (qi + 1) * block]
                remote(
                    piece, piece, g_send.at[delta - 1, qi], g_recv.at[delta - 1, qi], at_half(half)
                ).wait_recv()
                backward(h, h, half, qi, 2, False, True)

    finish_part(2, dv, 1.0)
    finish_part(3, dk, scale)
    filled = store_tiles(late_base, dot(normed, dproj[:, 2 * share :], (0, 0)).astype(BF16))
    clear(filled, total_chunks)
    reduce_start(late_ids)
    bias[0, 0:1, :] = jnp.sum(dproj[...].astype(F32), axis=0, keepdims=True)

    def bias_copy(stage):
        _, device = place_of(*all_streams[late_ids[0]][2][stage])
        return remote(
            bias.at[stage], bias_in.at[stage], b_send.at[stage], b_recv.at[stage], device
        )

    def bias_step(stage):
        bias_copy(stage).wait()
        bias[stage + 1] = bias[stage] + bias_in[stage]
        if stage + 1 < stages:
            bias_copy(stage + 1).start()

    bias_copy(0).start()

    mix_copy.wait_recv()
    result = (
        dot(mix_own[own_rows, :], out_w_ref[out_rows, :])
        + dot(mix_in[...], out_w_ref[out_rows_other, :])
        + out_b_ref[...]
        + seq_sc[...].astype(F32)
    )
    layer_ref[...] = jnp.where(present_at(mine), result, 0.0).astype(BF16)

    for turn in range(2 * stages + 1):
        advance(late_ids, turn)
        if turn < stages:
            bias_step(turn)
        if turn == stages:
            bias_ref[mine] = bias[stages]
            bias_own = bias_ref.at[mine]
            bias_final = remote(bias_own, bias_own, b_send.at[stages], b_recv.at[stages], partner)
            bias_final.start()
        advance(middle_ids, turn)
        advance(early_ids, turn + 2)

    bias_final.wait()
    for d in order:
        spot_copy(d).wait_send()
        row_copy(d).wait_send()
    cot_copy.wait_send()
    stat_copy.wait_send()
    mix_copy.wait_send()
    norm_copy(half).wait_send()
    for delta in range(1, halves):

        @pl.when(above(delta))
        def _():
            relay_spots(half, delta).wait_send()
            for d in [0] + order:
                relay(half, d, delta).wait_send()

        @pl.when(below(delta))
        def _():
            norm_copy(half - delta).wait_send()
            q_copy(delta).wait_send()
            for qi in range(2):
                g_copy(delta, qi).wait_send()


def unpack(full, bias_ref, layer_in, layer_ref, gpw_ref, gpb_ref, gow_ref, gob_ref, bases):
    model, width = gow_ref.shape[1], gow_ref.shape[0]
    share = width // 2
    layer_ref[...] = layer_in[...]

    for plane in range(2):
        for i, part in enumerate((0, 2, 1, 3)):
            low = part * width + plane * share
            gpb_ref[:, low : low + share] = bias_ref[plane, 0:1, i * share : (i + 1) * share]
        low = plane * (model // 2)
        gob_ref[:, low : low + model // 2] = bias_ref[plane, 1:2, : model // 2]

        def tile_of(base, height):
            return full[plane, base : base + height // ROWS].reshape(height, LANES)

        at = 0
        rows = slice(plane * share, (plane + 1) * share)
        for tile in range(model // LANES):
            gow_ref[rows, tile * LANES : (tile + 1) * LANES] = tile_of(at, share)
            at += share // ROWS
        size = model // ROWS
        per = share // LANES
        spots = (
            (0, at),
            (2, bases[1]),
            (1, bases[2]),
            (3, bases[2] + per * size),
        )
        for part, at in spots:
            for tile in range(per):
                low = part * width + plane * share + tile * LANES
                gpw_ref[:, low : low + LANES] = tile_of(at + tile * size, model)


def on_device(
    users,
    seqs,
    raw_events,
    target_user,
    target_place,
    send_counts,
    lengths,
    cotangent,
    encoder_in,
    encoder_out,
    proj_weight,
    proj_bias,
    out_weight,
    out_bias,
):
    slots = raw_events.shape[1]
    block, model = cotangent.shape[1], cotangent.shape[2]
    width = out_weight.shape[0]
    share = width // 2
    span = 2 * block
    halves = seqs // 2
    heads = share // HEAD
    others = max(halves - 1, 1)
    cap_pad = -(-(slots // users) // ROWS) * ROWS
    plans, stages, total = plan_of(users, seqs, groups_of(model, share))
    count = sum(len(plan) for plan in plans)
    vmem = pl.BlockSpec(memory_space=pltpu.VMEM)
    anywhere = pl.BlockSpec(memory_space=pl.ANY)
    smem = pl.BlockSpec(memory_space=pltpu.SMEM)
    dma = pltpu.SemaphoreType.DMA
    layer, full, bias = pl.pallas_call(
        functools.partial(kernel, users, seqs),
        out_shape=(
            jax.ShapeDtypeStruct((block, model), BF16),
            jax.ShapeDtypeStruct((2, total, ROWS, LANES), BF16),
            jax.ShapeDtypeStruct((2, 2, 4 * share), F32),
        ),
        in_specs=[anywhere, vmem, vmem, smem, smem] + [anywhere] * 4 + [vmem, anywhere, vmem],
        out_specs=(vmem,) * 3,
        scratch_shapes=[
            pltpu.VMEM((users, cap_pad, model), BF16),
            pltpu.VMEM((halves, users, cap_pad, model), BF16),
            pltpu.VMEM((users, 1, LANES), F32),
            pltpu.VMEM((halves, users, 1, LANES), F32),
            pltpu.VMEM((block, model), BF16),
            pltpu.VMEM((halves, 2, block, model), BF16),
            pltpu.VMEM((span, 4 * share), F32),
            pltpu.VMEM((span, share), BF16),
            pltpu.VMEM((halves, span, share), BF16),
            pltpu.VMEM((halves, span, share), BF16),
            pltpu.VMEM((halves, span, share), BF16),
            pltpu.VMEM((halves, span, share), BF16),
            pltpu.VMEM((halves, heads, span, span), BF16),
            pltpu.VMEM((halves, heads, span, span), F32),
            pltpu.VMEM((span, share), F32),
            pltpu.VMEM((span, share), F32),
            pltpu.VMEM((span, share), F32),
            pltpu.VMEM((span, share), F32),
            pltpu.VMEM((span, share), F32),
            pltpu.VMEM((span, 4 * share), BF16),
            pltpu.VMEM((4, span // LANES, 1, LANES), F32),
            pltpu.VMEM((4, span // LANES, 1, LANES), F32),
            pltpu.VMEM((span, share), BF16),
            pltpu.VMEM((block, share), BF16),
            pltpu.VMEM((total, ROWS, LANES), BF16),
            pltpu.VMEM((total, ROWS, LANES), BF16),
            pltpu.VMEM((stages + 1, 2, 4 * share), F32),
            pltpu.VMEM((stages, 2, 4 * share), F32),
            pltpu.VMEM(raw_events.shape[1:], BF16),
            pltpu.VMEM((2, block, model), BF16),
            pltpu.VMEM(encoder_in.shape, BF16),
            pltpu.VMEM(encoder_out.shape, BF16),
            pltpu.VMEM((model, 4 * share), BF16),
            pltpu.VMEM(out_weight.shape, BF16),
            dma((users,)),
            dma((users,)),
            dma((users,)),
            dma((users,)),
            dma((others, users)),
            dma((others, users)),
            dma((others,)),
            dma((others,)),
            dma((halves,)),
            dma((halves,)),
            dma((2,)),
            dma((2,)),
            dma((2,)),
            dma((others,)),
            dma((others,)),
            dma((others, 2)),
            dma((others, 2)),
            dma((count, stages)),
            dma((count, stages)),
            dma((count, stages)),
            dma((count, stages)),
            dma((count, 2)),
            dma((count, 2)),
            dma((stages + 1,)),
            dma((stages + 1,)),
            dma((9,)),
        ],
        compiler_params=pltpu.CompilerParams(
            collective_id=0, has_side_effects=True, vmem_limit_bytes=60000 * 1024
        ),
    )(
        raw_events[0],
        target_user,
        target_place,
        send_counts[0],
        lengths,
        cotangent[0],
        encoder_in,
        encoder_out,
        proj_weight,
        proj_bias[None],
        out_weight,
        out_bias[None],
    )
    layer_out, grad_pw, grad_pb, grad_ow, grad_ob = pl.pallas_call(
        functools.partial(unpack, bases=[plan[0][0] for plan in plans]),
        out_shape=(
            jax.ShapeDtypeStruct((block, model), BF16),
            jax.ShapeDtypeStruct((model, 4 * width), BF16),
            jax.ShapeDtypeStruct((1, 4 * width), F32),
            jax.ShapeDtypeStruct((width, model), BF16),
            jax.ShapeDtypeStruct((1, model), F32),
        ),
        in_specs=[vmem] * 3,
        out_specs=(vmem,) * 5,
    )(full, bias, layer)
    return layer_out[None], grad_pw, grad_pb[0], grad_ow, grad_ob[0]


def solution(mesh):
    placed = (
        P("seq", "users", None),
        P("seq", "users"),
        P("seq", "users"),
        P("seq", "users", None),
        P("users"),
        P("users", "seq", None),
        P(),
        P(),
        P(),
        P(),
        P(),
        P(),
    )
    return jax.shard_map(
        functools.partial(on_device, mesh.shape["users"], mesh.shape["seq"]),
        mesh=mesh,
        in_specs=placed,
        out_specs=(P("users", "seq", None), P(), P(), P(), P()),
        check_vma=False,
    )
```

```python
import functools

import jax
import jax.numpy as jnp
from jax import lax
from jax.experimental import pallas as pl
from jax.experimental.pallas import tpu as pltpu
from jax.sharding import PartitionSpec as P

HEAD = 64
EPSILON = 1e-05
LANES = 128
ROWS = 16
RESIDENT = 320
F32 = jnp.float32
BF16 = jnp.bfloat16


def sigmoid(values):
    return 0.5 * jnp.tanh(0.5 * values) + 0.5


def silu(values):
    return values * sigmoid(values)


def silu_grad(values):
    gate = sigmoid(values)
    return gate * (1.0 + values * (1.0 - gate))


def layer_norm(values):
    center = values - jnp.mean(values, axis=-1, keepdims=True)
    inverse = lax.rsqrt(jnp.mean(center * center, axis=-1, keepdims=True) + EPSILON)
    return center * inverse, inverse


def dot(a, b, contract=(1, 0)):
    return lax.dot_general(
        a, b, (((contract[0],), (contract[1],)), ((), ())), preferred_element_type=F32
    )


def flip(index, bit):
    return index + bit * (1 - 2 * ((index // bit) % 2))


def flip_all(index, delta):
    bit = 1
    while bit <= delta:
        if delta & bit:
            index = flip(index, bit)
        bit *= 2
    return index


def plan_of(users, seqs, groups):
    near, far = [], []
    bit = 1
    while bit < users:
        near.append(("users", bit))
        bit *= 2
    bit = 2
    while bit < seqs:
        far.append(("seq", bit))
        bit *= 2
    devices = users * seqs // 2
    plans = []
    base = 0
    for chunks, most, across_first in groups:
        each = -(-chunks // devices)
        if across_first:
            turn = (far + near)[:3]
            tail = (far + near)[3:]
        else:
            turn = near[:2]
            tail = near[2:] + far
        streams = []
        for i in range(most):
            share = (each + most - 1 - i) // most
            if share == 0:
                continue
            k = i % len(turn)
            streams.append((base, share * devices, turn[k:] + turn[:k] + tail))
            base += share * devices
        plans.append(streams)
    return plans, len(near) + len(far), base


def groups_of(model, share):
    tile = ROWS * LANES
    return (
        (2 * model * share // tile, 2, False),
        (model * share // tile, 2, False),
        (2 * model * share // tile, 4, True),
    )


def kernel(
    users,
    seqs,
    raw_hbm,
    user_ref,
    place_ref,
    counts_ref,
    length_hbm,
    cot_hbm,
    enc_in_hbm,
    enc_out_hbm,
    proj_w_hbm,
    proj_b_ref,
    out_w_hbm,
    out_b_ref,
    layer_ref,
    full,
    bias_ref,
    send_buf,
    rows_sc,
    spot_out,
    spot_in,
    seq_sc,
    norm_sc,
    proj_sc,
    gate_sc,
    v_sc,
    k_sc,
    qb,
    gb,
    w_sc,
    s_sc,
    att,
    dq,
    dk,
    dv,
    d_mix,
    dproj,
    stat_out,
    stat_in,
    mix_own,
    mix_in,
    work,
    landing,
    bias,
    bias_in,
    raw_ref,
    cots,
    enc_in_ref,
    enc_out_ref,
    proj_w_ref,
    out_w_ref,
    a2a_send,
    a2a_recv,
    spot_send,
    spot_recv,
    x_send,
    x_recv,
    xs_send,
    xs_recv,
    n_send,
    n_recv,
    cot_sem,
    stat_sem,
    mix_sem,
    q_send,
    q_recv,
    g_send,
    g_recv,
    rs_send,
    rs_recv,
    ag_send,
    ag_recv,
    core_send,
    core_recv,
    b_send,
    b_recv,
    in_sem,
    length_sm,
    length_sem,
):
    me_u = lax.axis_index("users")
    me_s = lax.axis_index("seq")
    MESH = pl.DeviceIdType.MESH
    slots, model = raw_ref.shape
    block = layer_ref.shape[0]
    span = 2 * block
    width = out_w_ref.shape[0]
    share = width // 2
    pairs = share // LANES
    cap_pad = send_buf.shape[1]
    halves = seqs // 2
    scale = HEAD ** (-0.5)
    mine = me_s % 2
    half = me_s // 2
    partner = (me_u, flip(me_s, 1))

    def at_half(h):
        return (me_u, h * 2 + mine)

    def remote(source, target, send_sem, recv_sem, device):
        return pltpu.make_async_remote_copy(
            src_ref=source,
            dst_ref=target,
            send_sem=send_sem,
            recv_sem=recv_sem,
            device_id=device,
            device_id_type=MESH,
        )

    barrier = pltpu.get_barrier_semaphore()
    greeted = [(lax.rem(me_u + delta, users), me_s) for delta in range(1, users)]
    greeted += [partner]
    greeted += [at_half(lax.rem(half + delta, halves)) for delta in range(1, halves)]
    for device in greeted:
        pl.semaphore_signal(barrier, inc=1, device_id=device, device_id_type=MESH)

    def own_columns(part):
        return pl.ds(pl.multiple_of(part * width + mine * share, LANES), share)

    length_load = pltpu.make_async_copy(length_hbm, length_sm, length_sem)
    length_load.start()
    parts = (0, 2, 1, 3)
    loads = [
        pltpu.make_async_copy(source, target, in_sem.at[i])
        for i, (source, target) in enumerate(
            [
                (raw_hbm, raw_ref),
                (cot_hbm, cots.at[mine]),
                (out_w_hbm, out_w_ref),
                (enc_in_hbm, enc_in_ref),
                (enc_out_hbm, enc_out_ref),
            ]
            + [
                (
                    proj_w_hbm.at[:, own_columns(part)],
                    proj_w_ref.at[:, i * share : (i + 1) * share],
                )
                for i, part in enumerate(parts)
            ]
        )
    ]
    for load in loads:
        load.start()

    target = user_ref[...]
    lane_row = lax.broadcasted_iota(jnp.int32, (1, slots), 1)
    first = jnp.zeros((1, slots), jnp.int32)
    total = jnp.int32(0)
    for u in range(users):
        first = jnp.where(target == u, total, first)
        total = total + counts_ref[0, u]
    flat = jnp.where(lane_row < total, target * cap_pad + lane_row - first, -1)
    hot = lax.broadcasted_iota(jnp.int32, (users * cap_pad, slots), 0) == flat
    local_place = (place_ref[...] - me_s * block + 1).astype(F32)
    spots = jnp.sum(jnp.where(hot, local_place, 0.0), axis=1, keepdims=True) - 1.0
    diagonal = lax.broadcasted_iota(
        jnp.int32, (users, cap_pad, LANES), 1
    ) == lax.broadcasted_iota(jnp.int32, (users, cap_pad, LANES), 2)
    spot_out[...] = jnp.sum(
        jnp.where(diagonal, spots.reshape(users, cap_pad, 1), 0.0), axis=1, keepdims=True
    )
    loads[0].wait()
    bucket = dot(hot.astype(F32).astype(BF16), raw_ref[...]).astype(BF16)
    send_buf[...] = bucket.reshape(users, cap_pad, model)

    pl.semaphore_wait(barrier, len(greeted))

    order = list(range(1, users))

    def spot_copy(d):
        peer = flip_all(me_u, d)
        return remote(
            spot_out.at[peer], spot_in.at[half, me_u], spot_send.at[d], spot_recv.at[d], (peer, me_s)
        )

    def row_copy(d):
        peer = flip_all(me_u, d)
        return remote(
            send_buf.at[peer], rows_sc.at[half, me_u], a2a_send.at[d], a2a_recv.at[d], (peer, me_s)
        )

    def relay(h, d, delta):
        source = flip_all(me_u, d)
        held = send_buf.at[source] if d == 0 else rows_sc.at[h, source]
        return remote(
            held,
            rows_sc.at[h, source],
            x_send.at[delta - 1, d],
            x_recv.at[delta - 1, d],
            at_half(h + delta),
        )

    def relay_spots(h, delta):
        return remote(
            spot_in.at[h],
            spot_in.at[h],
            xs_send.at[delta - 1],
            xs_recv.at[delta - 1],
            at_half(h + delta),
        )

    def above(delta):
        return half + delta < halves

    def below(delta):
        return half >= delta

    for d in order:
        spot_copy(d).start()
    for d in order:
        row_copy(d).start()
    for delta in range(1, halves):

        @pl.when(above(delta))
        def _():
            relay(half, 0, delta).start()

    loads[1].wait()
    cot_copy = remote(cots.at[mine], cots.at[mine], cot_sem.at[0], cot_sem.at[1], partner)
    cot_copy.start()
    rows_sc[half, me_u] = send_buf[me_u]
    spot_in[half, me_u] = spot_out[me_u]

    length_load.wait()
    length = length_sm[0]
    rows = lax.broadcasted_iota(jnp.int32, (block, 1), 0)

    def block_rows(index):
        return pl.ds(pl.multiple_of(index * block, block), block)

    own_rows, other_rows = block_rows(mine), block_rows(1 - mine)

    def present_at(index):
        return (half * 2 + index) * block + rows < length

    out_rows = pl.ds(pl.multiple_of(mine * share, LANES), share)
    out_rows_other = pl.ds(pl.multiple_of((1 - mine) * share, LANES), share)
    loads[2].wait()

    def mask_cot(index):
        d_out = jnp.where(
            present_at(index), cots[index], jnp.zeros((block, model), BF16)
        )
        d_mix[block_rows(index), :] = dot(d_out, out_w_ref[out_rows, :], (1, 1))

    mask_cot(mine)
    for load in loads[3:]:
        load.wait()
    bias_row = jnp.concatenate([proj_b_ref[:, own_columns(part)] for part in parts], axis=1)
    att[...] = jnp.zeros_like(att)
    dq[...] = jnp.zeros_like(dq)
    dk[...] = jnp.zeros_like(dk)
    dv[...] = jnp.zeros_like(dv)
    cot_copy.wait_recv()
    mask_cot(1 - mine)

    for d in order:
        row_copy(d).wait_recv()
        for delta in range(1, halves):

            @pl.when(above(delta))
            def _():
                relay(half, d, delta).start()

    for d in order:
        spot_copy(d).wait_recv()
    for delta in range(1, halves):

        @pl.when(above(delta))
        def _():
            relay_spots(half, delta).start()

    def ingest(h):
        arrived = rows_sc[h].reshape(users * cap_pad, model)
        where_to = jnp.sum(jnp.where(diagonal, spot_in[h], 0.0), axis=2, keepdims=True)
        where_to = where_to.reshape(users * cap_pad, 1).astype(jnp.int32)
        placed = (
            lax.broadcasted_iota(jnp.int32, (users * cap_pad, block), 1) == where_to
        ).astype(F32).astype(BF16)
        events = dot(placed, arrived, (0, 0)).astype(BF16)
        hidden = silu(dot(events, enc_in_ref[...])).astype(BF16)
        sequence = dot(hidden, enc_out_ref[...]).astype(BF16)
        norm_sc[h, mine] = layer_norm(sequence.astype(F32))[0].astype(BF16)
        return sequence

    def norm_copy(h):
        own = norm_sc.at[h, mine]
        return remote(own, own, n_send.at[h], n_recv.at[h], partner)

    seq_sc[...] = ingest(half)
    norm_copy(half).start()

    def project(index):
        at = block_rows(index)
        projected = dot(norm_sc[half, index], proj_w_ref[...]) + bias_row
        proj_sc[at, :] = projected
        gates = silu(projected).astype(BF16)
        gate_sc[at, :] = gates[:, :share]
        qb[half, at, :] = gates[:, share : 2 * share]
        v_sc[half, at, :] = gates[:, 2 * share : 3 * share]
        k_sc[half, at, :] = gates[:, 3 * share :]

    def project_low(h, index):
        at = block_rows(index)
        gates = silu(
            dot(norm_sc[h, index], proj_w_ref[:, 2 * share :]) + bias_row[:, 2 * share :]
        ).astype(BF16)
        v_sc[h, at, :] = gates[:, :share]
        k_sc[h, at, :] = gates[:, share:]

    def half_of(values, hh):
        zero = jnp.zeros_like(values)
        low = lax.broadcasted_iota(jnp.int32, values.shape, 1) < HEAD
        return jnp.where(low, values, zero) if hh == 0 else jnp.where(low, zero, values)

    def lanes(p):
        return slice(p * LANES, (p + 1) * LANES)

    def merge(low, high):
        keep = lax.broadcasted_iota(jnp.int32, low.shape, 1) < HEAD
        return jnp.where(keep, low, high)

    def scores_of(slot, q_half, qi, k_half, ki):
        qr, kr = block_rows(qi), block_rows(ki)
        bound = jnp.minimum((q_half * 2 + qi) * block + rows, length - 1)
        bound = bound - (k_half * 2 + ki) * block
        allowed = lax.broadcasted_iota(jnp.int32, (block, block), 1) <= bound
        for p in range(pairs):
            queries = qb[q_half, qr, lanes(p)]
            keys = k_sc[k_half, kr, lanes(p)]
            for hh in range(2):
                score = dot(half_of(queries, hh), keys, (1, 1)) * scale
                gate = sigmoid(score)
                plain = score * gate
                w_sc[slot, 2 * p + hh, qr, kr] = jnp.where(allowed, plain, 0.0).astype(BF16)
                s_sc[slot, 2 * p + hh, qr, kr] = jnp.where(
                    allowed, gate + plain * (1.0 - gate), 0.0
                )

    def attend(slot, qi, k_half, ki):
        qr, kr = block_rows(qi), block_rows(ki)
        for p in range(pairs):
            values = v_sc[k_half, kr, lanes(p)]
            att[qr, lanes(p)] = att[qr, lanes(p)] + merge(
                dot(w_sc[slot, 2 * p, qr, kr], values), dot(w_sc[slot, 2 * p + 1, qr, kr], values)
            )

    project(mine)

    def own_block(qi, ki):
        scores_of(half, half, qi, half, ki)
        attend(half, qi, half, ki)

    own_block(mine, mine)

    norm_copy(half).wait_recv()
    project(1 - mine)

    def q_copy(delta):
        return remote(
            qb.at[half], qb.at[half], q_send.at[delta - 1], q_recv.at[delta - 1], at_half(half - delta)
        )

    for delta in range(1, halves):

        @pl.when(below(delta))
        def _():
            q_copy(delta).start()

    own_block(1 - mine, 1 - mine)
    own_block(1, 0)

    for delta in range(1, halves):

        @pl.when(below(delta))
        def _():
            h = half - delta
            relay_spots(h, delta).wait_recv()
            for d in [0] + order:
                relay(h, d, delta).wait_recv()

    for delta in range(1, halves):

        @pl.when(below(delta))
        def _():
            h = half - delta
            ingest(h)
            norm_copy(h).start()
            for ki in (mine, 1 - mine):
                if ki is not mine:
                    norm_copy(h).wait_recv()
                project_low(h, ki)
                for qi in range(2):
                    scores_of(h, half, qi, h, ki)
                    attend(h, qi, h, ki)

    attended = att[...]
    gate_u = gate_sc[...].astype(F32)
    d_mixed = d_mix[...]
    d_onorm = d_mixed * gate_u
    own_mean = jnp.mean(attended, axis=-1, keepdims=True)
    center = attended - own_mean
    facts = (
        own_mean,
        jnp.sum(center * center, axis=-1, keepdims=True),
        jnp.sum(d_onorm, axis=-1, keepdims=True),
        jnp.sum(d_onorm * center, axis=-1, keepdims=True),
    )
    tall = span // LANES
    square = lax.broadcasted_iota(jnp.int32, (tall, LANES, LANES), 1) == lax.broadcasted_iota(
        jnp.int32, (tall, LANES, LANES), 2
    )
    for i, fact in enumerate(facts):
        stat_out[i] = jnp.sum(
            jnp.where(square, fact.reshape(tall, LANES, 1), 0.0), axis=1, keepdims=True
        )
    stat_copy = remote(stat_out, stat_in, stat_sem.at[0], stat_sem.at[1], partner)
    stat_copy.start()

    stat_copy.wait_recv()
    theirs = [
        jnp.sum(jnp.where(square, stat_in[i], 0.0), axis=2, keepdims=True).reshape(span, 1)
        for i in range(len(facts))
    ]
    mean = 0.5 * (own_mean + theirs[0])
    gap = own_mean - theirs[0]
    variance = (facts[1] + theirs[1] + gap * gap * (0.5 * share)) / width
    inverse = lax.rsqrt(variance + EPSILON)
    mean_d = (facts[2] + theirs[2]) / width
    mean_do = (
        (facts[3] + theirs[3] + (own_mean - mean) * facts[2] + (theirs[0] - mean) * theirs[2])
        * inverse
        / width
    )
    onorm = (attended - mean) * inverse
    d_att = ((d_onorm - mean_d - onorm * mean_do) * inverse).astype(BF16)
    gb[half] = d_att

    def g_copy(delta, qi):
        piece = gb.at[half, qi * block : (qi + 1) * block]
        return remote(
            piece, piece, g_send.at[delta - 1, qi], g_recv.at[delta - 1, qi], at_half(half - delta)
        )

    for delta in range(1, halves):

        @pl.when(below(delta))
        def _():
            for qi in range(2):
                g_copy(delta, qi).start()

    mixed = (onorm * gate_u).astype(BF16)
    mix_own[...] = mixed
    mix_copy = remote(mix_own.at[other_rows], mix_in, mix_sem.at[0], mix_sem.at[1], partner)
    mix_copy.start()
    dproj[:, :share] = (d_mixed * onorm * silu_grad(proj_sc[:, :share])).astype(BF16)
    positions = lax.broadcasted_iota(jnp.int32, (span, 1), 0)
    present = half * span + positions < length
    d_out = jnp.where(present, cots[...].reshape(span, model), jnp.zeros((span, model), BF16))
    normed = norm_sc[half].reshape(span, model)
    column = jnp.sum(d_out.astype(F32), axis=0, keepdims=True)
    bias[0] = jnp.zeros_like(bias[0])
    bias[0, 1:2, : model // 2] = jnp.where(
        mine == 0, column[:, : model // 2], column[:, model // 2 :]
    )
    (early, middle, late), stages, total_chunks = plan_of(users, seqs, groups_of(model, share))
    middle_base, late_base = middle[0][0], late[0][0]

    def store_tiles(base, values):
        height = values.shape[0] // ROWS
        for tile in range(values.shape[1] // LANES):
            work[base + tile * height : base + (tile + 1) * height] = values[
                :, tile * LANES : (tile + 1) * LANES
            ].reshape(height, ROWS, LANES)
        return base + values.shape[0] * values.shape[1] // (ROWS * LANES)

    def clear(base, stop):
        if base < stop:
            work[base:stop] = jnp.zeros((stop - base, ROWS, LANES), BF16)

    filled = store_tiles(0, dot(mixed, d_out, (0, 0)).astype(BF16))
    filled = store_tiles(filled, dot(normed, dproj[:, :share], (0, 0)).astype(BF16))
    clear(filled, middle_base)

    def place_of(axis, bit):
        own = me_s if axis == "seq" else me_u
        peer = flip(own, bit)
        device = (me_u, peer) if axis == "seq" else (peer, me_s)
        return (own // bit) % 2, device

    all_streams = early + middle + late
    starts = []
    for base, size, bit_order in all_streams:
        offsets = [base]
        for stage in range(stages):
            side, _ = place_of(*bit_order[stage])
            offsets.append(offsets[stage] + side * (size >> (stage + 1)))
        starts.append(offsets)
    landings = []
    landing_at = 0
    for base, size, _ in all_streams:
        offsets = []
        for stage in range(stages):
            offsets.append(landing_at)
            landing_at += size >> (stage + 1)
        landings.append(offsets)
    early_ids = list(range(len(early)))
    middle_ids = list(range(len(early), len(early) + len(middle)))
    late_ids = list(range(len(early) + len(middle), len(all_streams)))

    def reduce_copy(i, stage):
        base, size, bit_order = all_streams[i]
        side, device = place_of(*bit_order[stage])
        part = size >> (stage + 1)
        start = starts[i][stage]
        return (
            remote(
                work.at[pl.ds(start + (1 - side) * part, part)],
                landing.at[pl.ds(landings[i][stage], part)],
                rs_send.at[i, stage],
                rs_recv.at[i, stage],
                device,
            ),
            start + side * part,
            part,
        )

    def gather_copy(i, stage):
        base, size, bit_order = all_streams[i]
        _, device = place_of(*bit_order[stage])
        own = full.at[mine, pl.ds(starts[i][stage + 1], size >> (stage + 1))]
        return remote(own, own, ag_send.at[i, stage], ag_recv.at[i, stage], device)

    def core_copy(i, second):
        base, size, bit_order = all_streams[i]
        side, _ = place_of(*bit_order[0])
        part = size >> 1
        start = base + (1 - side) * part if second else base + side * part
        own = full.at[mine, pl.ds(start, part)]
        return remote(own, own, core_send.at[i, second], core_recv.at[i, second], partner)

    def reduce_start(ids):
        for i in ids:
            reduce_copy(i, 0)[0].start()

    def reduce_step(ids, stage):
        for i in ids:
            copy, keep, part = reduce_copy(i, stage)
            copy.wait()
            at = landings[i][stage]
            summed = (
                work[pl.ds(keep, part)].astype(F32) + landing[at : at + part].astype(F32)
            ).astype(BF16)
            if stage + 1 < stages:
                work[pl.ds(keep, part)] = summed
                reduce_copy(i, stage + 1)[0].start()
            else:
                full[mine, pl.ds(keep, part)] = summed
                gather_copy(i, stage).start()
                if stage == 0:
                    core_copy(i, 0).start()

    def gather_step(ids, stage):
        for i in ids:
            gather_copy(i, stage).wait()
            if stage > 0:
                gather_copy(i, stage - 1).start()
                if stage == 1:
                    core_copy(i, 0).start()
            else:
                core_copy(i, 1).start()

    def core_finish(ids):
        for i in ids:
            core_copy(i, 0).wait()
            core_copy(i, 1).wait()

    def advance(ids, turn):
        if turn < stages:
            reduce_step(ids, turn)
        elif turn < 2 * stages:
            gather_step(ids, 2 * stages - 1 - turn)
        elif turn == 2 * stages:
            core_finish(ids)

    reduce_start(early_ids)

    for delta in range(1, halves):

        @pl.when(above(delta))
        def _():
            h = half + delta
            remote(
                qb.at[h], qb.at[h], q_send.at[delta - 1], q_recv.at[delta - 1], at_half(half)
            ).wait_recv()
            for qi in range(2):
                for ki in range(2):
                    scores_of(h, h, qi, half, ki)

    def backward(slot, q_half, k_half, qi, keys_to, query_side, key_side):
        qr = slice(qi * block, (qi + 1) * block)
        kr = slice(0, keys_to * block)
        for p in range(pairs):
            at = lanes(p)
            grads = gb[q_half, qr, at]
            values = v_sc[k_half, kr, at]
            d_scores = []
            for hh in range(2):
                d_weight = dot(half_of(grads, hh), values, (1, 1))
                d_scores.append((d_weight * s_sc[slot, 2 * p + hh, qr, kr]).astype(BF16))
            if query_side:
                keys = k_sc[k_half, kr, at]
                dq[qr, at] = dq[qr, at] + merge(dot(d_scores[0], keys), dot(d_scores[1], keys))
            if key_side:
                queries = qb[q_half, qr, at]
                dk[kr, at] = dk[kr, at] + merge(
                    dot(d_scores[0], queries, (0, 0)), dot(d_scores[1], queries, (0, 0))
                )
                dv[kr, at] = dv[kr, at] + merge(
                    dot(w_sc[slot, 2 * p, qr, kr], grads, (0, 0)),
                    dot(w_sc[slot, 2 * p + 1, qr, kr], grads, (0, 0)),
                )

    for qi in range(2):
        backward(half, half, half, qi, qi + 1, True, True)

    for delta in range(1, halves):

        @pl.when(below(delta))
        def _():
            h = half - delta
            for qi in range(2):
                backward(h, half, h, qi, 2, True, False)

    def finish_part(index, buf, factor):
        at = slice(index * share, (index + 1) * share)
        dproj[:, at] = (buf[...] * factor * silu_grad(proj_sc[:, at])).astype(BF16)

    finish_part(1, dq, scale)
    filled = store_tiles(
        middle_base, dot(normed, dproj[:, share : 2 * share], (0, 0)).astype(BF16)
    )
    clear(filled, late_base)
    reduce_start(middle_ids)

    @pl.when(above(1))
    def _():
        advance(early_ids, 0)
        advance(early_ids, 1)

    for delta in range(1, halves):

        @pl.when(above(delta))
        def _():
            h = half + delta
            for qi in range(2):
                piece = gb.at[h, qi * block : (qi + 1) * block]
                remote(
                    piece, piece, g_send.at[delta - 1, qi], g_recv.at[delta - 1, qi], at_half(half)
                ).wait_recv()
                backward(h, h, half, qi, 2, False, True)

    finish_part(2, dv, 1.0)
    finish_part(3, dk, scale)
    filled = store_tiles(late_base, dot(normed, dproj[:, 2 * share :], (0, 0)).astype(BF16))
    clear(filled, total_chunks)
    reduce_start(late_ids)
    bias[0, 0:1, :] = jnp.sum(dproj[...].astype(F32), axis=0, keepdims=True)

    def bias_copy(stage):
        _, device = place_of(*all_streams[late_ids[0]][2][stage])
        return remote(
            bias.at[stage], bias_in.at[stage], b_send.at[stage], b_recv.at[stage], device
        )

    def bias_step(stage):
        bias_copy(stage).wait()
        bias[stage + 1] = bias[stage] + bias_in[stage]
        if stage + 1 < stages:
            bias_copy(stage + 1).start()

    bias_copy(0).start()

    mix_copy.wait_recv()
    result = (
        dot(mix_own[own_rows, :], out_w_ref[out_rows, :])
        + dot(mix_in[...], out_w_ref[out_rows_other, :])
        + out_b_ref[...]
        + seq_sc[...].astype(F32)
    )
    layer_ref[...] = jnp.where(present_at(mine), result, 0.0).astype(BF16)

    @pl.when(jnp.logical_not(above(1)))
    def _():
        advance(early_ids, 0)
        advance(early_ids, 1)

    for turn in range(2 * stages + 1):
        advance(late_ids, turn)
        if turn < stages:
            bias_step(turn)
        if turn == stages:
            bias_ref[mine] = bias[stages]
            bias_own = bias_ref.at[mine]
            bias_final = remote(bias_own, bias_own, b_send.at[stages], b_recv.at[stages], partner)
            bias_final.start()
        advance(middle_ids, turn)
        advance(early_ids, turn + 2)

    bias_final.wait()
    for d in order:
        spot_copy(d).wait_send()
        row_copy(d).wait_send()
    cot_copy.wait_send()
    stat_copy.wait_send()
    mix_copy.wait_send()
    norm_copy(half).wait_send()
    for delta in range(1, halves):

        @pl.when(above(delta))
        def _():
            relay_spots(half, delta).wait_send()
            for d in [0] + order:
                relay(half, d, delta).wait_send()

        @pl.when(below(delta))
        def _():
            norm_copy(half - delta).wait_send()
            q_copy(delta).wait_send()
            for qi in range(2):
                g_copy(delta, qi).wait_send()


def unpack(full, bias_ref, layer_in, layer_ref, gpw_ref, gpb_ref, gow_ref, gob_ref, bases):
    model, width = gow_ref.shape[1], gow_ref.shape[0]
    share = width // 2
    layer_ref[...] = layer_in[...]

    for plane in range(2):
        for i, part in enumerate((0, 2, 1, 3)):
            low = part * width + plane * share
            gpb_ref[:, low : low + share] = bias_ref[plane, 0:1, i * share : (i + 1) * share]
        low = plane * (model // 2)
        gob_ref[:, low : low + model // 2] = bias_ref[plane, 1:2, : model // 2]

        def tile_of(base, height):
            return full[plane, base : base + height // ROWS].reshape(height, LANES)

        at = 0
        rows = slice(plane * share, (plane + 1) * share)
        for tile in range(model // LANES):
            gow_ref[rows, tile * LANES : (tile + 1) * LANES] = tile_of(at, share)
            at += share // ROWS
        size = model // ROWS
        per = share // LANES
        spots = (
            (0, at),
            (2, bases[1]),
            (1, bases[2]),
            (3, bases[2] + per * size),
        )
        for part, at in spots:
            for tile in range(per):
                low = part * width + plane * share + tile * LANES
                gpw_ref[:, low : low + LANES] = tile_of(at + tile * size, model)


def on_device(
    users,
    seqs,
    raw_events,
    target_user,
    target_place,
    send_counts,
    lengths,
    cotangent,
    encoder_in,
    encoder_out,
    proj_weight,
    proj_bias,
    out_weight,
    out_bias,
):
    slots = raw_events.shape[1]
    block, model = cotangent.shape[1], cotangent.shape[2]
    width = out_weight.shape[0]
    share = width // 2
    span = 2 * block
    halves = seqs // 2
    heads = share // HEAD
    others = max(halves - 1, 1)
    cap_pad = -(-(slots // users) // ROWS) * ROWS
    plans, stages, total = plan_of(users, seqs, groups_of(model, share))
    count = sum(len(plan) for plan in plans)
    vmem = pl.BlockSpec(memory_space=pltpu.VMEM)
    anywhere = pl.BlockSpec(memory_space=pl.ANY)
    smem = pl.BlockSpec(memory_space=pltpu.SMEM)
    dma = pltpu.SemaphoreType.DMA
    resident = 2 * total <= RESIDENT
    result = pltpu.VMEM if resident else jax.ShapeDtypeStruct
    layer, full, bias = pl.pallas_call(
        functools.partial(kernel, users, seqs),
        out_shape=(
            result((block, model), BF16),
            result((2, total, ROWS, LANES), BF16),
            result((2, 2, 4 * share), F32),
        ),
        in_specs=[anywhere, vmem, vmem, smem, pl.BlockSpec(memory_space=pltpu.HBM)]
        + [anywhere] * 4 + [vmem, anywhere, vmem],
        out_specs=(vmem,) * 3,
        scratch_shapes=[
            pltpu.VMEM((users, cap_pad, model), BF16),
            pltpu.VMEM((halves, users, cap_pad, model), BF16),
            pltpu.VMEM((users, 1, LANES), F32),
            pltpu.VMEM((halves, users, 1, LANES), F32),
            pltpu.VMEM((block, model), BF16),
            pltpu.VMEM((halves, 2, block, model), BF16),
            pltpu.VMEM((span, 4 * share), F32),
            pltpu.VMEM((span, share), BF16),
            pltpu.VMEM((halves, span, share), BF16),
            pltpu.VMEM((halves, span, share), BF16),
            pltpu.VMEM((halves, span, share), BF16),
            pltpu.VMEM((halves, span, share), BF16),
            pltpu.VMEM((halves, heads, span, span), BF16),
            pltpu.VMEM((halves, heads, span, span), F32),
            pltpu.VMEM((span, share), F32),
            pltpu.VMEM((span, share), F32),
            pltpu.VMEM((span, share), F32),
            pltpu.VMEM((span, share), F32),
            pltpu.VMEM((span, share), F32),
            pltpu.VMEM((span, 4 * share), BF16),
            pltpu.VMEM((4, span // LANES, 1, LANES), F32),
            pltpu.VMEM((4, span // LANES, 1, LANES), F32),
            pltpu.VMEM((span, share), BF16),
            pltpu.VMEM((block, share), BF16),
            pltpu.VMEM((total, ROWS, LANES), BF16),
            pltpu.VMEM((total, ROWS, LANES), BF16),
            pltpu.VMEM((stages + 1, 2, 4 * share), F32),
            pltpu.VMEM((stages, 2, 4 * share), F32),
            pltpu.VMEM(raw_events.shape[1:], BF16),
            pltpu.VMEM((2, block, model), BF16),
            pltpu.VMEM(encoder_in.shape, BF16),
            pltpu.VMEM(encoder_out.shape, BF16),
            pltpu.VMEM((model, 4 * share), BF16),
            pltpu.VMEM(out_weight.shape, BF16),
            dma((users,)),
            dma((users,)),
            dma((users,)),
            dma((users,)),
            dma((others, users)),
            dma((others, users)),
            dma((others,)),
            dma((others,)),
            dma((halves,)),
            dma((halves,)),
            dma((2,)),
            dma((2,)),
            dma((2,)),
            dma((others,)),
            dma((others,)),
            dma((others, 2)),
            dma((others, 2)),
            dma((count, stages)),
            dma((count, stages)),
            dma((count, stages)),
            dma((count, stages)),
            dma((count, 2)),
            dma((count, 2)),
            dma((stages + 1,)),
            dma((stages + 1,)),
            dma((9,)),
            pltpu.SMEM(lengths.shape, jnp.int32),
            dma,
        ],
        compiler_params=pltpu.CompilerParams(
            collective_id=0, has_side_effects=True, vmem_limit_bytes=60000 * 1024
        ),
    )(
        raw_events[0],
        target_user,
        target_place,
        send_counts[0],
        lengths,
        cotangent[0],
        encoder_in,
        encoder_out,
        proj_weight,
        proj_bias[None],
        out_weight,
        out_bias[None],
    )
    held = (full, bias, layer)
    if resident:
        held = [pltpu.with_memory_space_constraint(array, pltpu.VMEM) for array in held]
    layer_out, grad_pw, grad_pb, grad_ow, grad_ob = pl.pallas_call(
        functools.partial(unpack, bases=[plan[0][0] for plan in plans]),
        out_shape=(
            jax.ShapeDtypeStruct((block, model), BF16),
            jax.ShapeDtypeStruct((model, 4 * width), BF16),
            jax.ShapeDtypeStruct((1, 4 * width), F32),
            jax.ShapeDtypeStruct((width, model), BF16),
            jax.ShapeDtypeStruct((1, model), F32),
        ),
        in_specs=[vmem] * 3,
        out_specs=(vmem,) * 5,
    )(*held)
    return layer_out[None], grad_pw, grad_pb[0], grad_ow, grad_ob[0]


def solution(mesh):
    placed = (
        P("seq", "users", None),
        P("seq", "users"),
        P("seq", "users"),
        P("seq", "users", None),
        P("users"),
        P("users", "seq", None),
        P(),
        P(),
        P(),
        P(),
        P(),
        P(),
    )
    return jax.shard_map(
        functools.partial(on_device, mesh.shape["users"], mesh.shape["seq"]),
        mesh=mesh,
        in_specs=placed,
        out_specs=(P("users", "seq", None), P(), P(), P(), P()),
        check_vma=False,
    )
```

```python
import functools

import jax
import jax.numpy as jnp
from jax import lax
from jax.experimental import pallas as pl
from jax.experimental.pallas import tpu as pltpu
from jax.sharding import PartitionSpec as P

HEAD = 64
EPSILON = 1e-05
LANES = 128
ROWS = 16
RESIDENT = 320
QUAD = (1, 2, 3)
F32 = jnp.float32
BF16 = jnp.bfloat16


def sigmoid(values):
    return 0.5 * jnp.tanh(0.5 * values) + 0.5


def silu(values):
    return values * sigmoid(values)


def silu_grad(values):
    gate = sigmoid(values)
    return gate * (1.0 + values * (1.0 - gate))


def layer_norm(values):
    center = values - jnp.mean(values, axis=-1, keepdims=True)
    inverse = lax.rsqrt(jnp.mean(center * center, axis=-1, keepdims=True) + EPSILON)
    return center * inverse, inverse


def dot(a, b, contract=(1, 0)):
    return lax.dot_general(
        a, b, (((contract[0],), (contract[1],)), ((), ())), preferred_element_type=F32
    )


def flip(index, bit):
    return index + bit * (1 - 2 * ((index // bit) % 2))


def flip_all(index, delta):
    bit = 1
    while bit <= delta:
        if delta & bit:
            index = flip(index, bit)
        bit *= 2
    return index


def plan_of(users, seqs, groups):
    near, far = [], []
    bit = 1
    while bit < users:
        near.append(("users", bit))
        bit *= 2
    bit = 2
    while bit < seqs:
        far.append(("seq", bit))
        bit *= 2
    devices = users * seqs // 2
    plans = []
    base = 0
    for chunks, most, across_first in groups:
        each = -(-chunks // devices)
        if across_first:
            turn, tail = far + near[:-2], near[-2:]
        else:
            turn, tail = [], near[:-2] + far + near[-2:]
        streams = []
        for i in range(most):
            share = (each + most - 1 - i) // most
            if share == 0:
                continue
            k = i % max(len(turn), 1)
            streams.append((base, share * devices, turn[k:] + turn[:k] + tail))
            base += share * devices
        plans.append(streams)
    return plans, len(near) + len(far), base


def groups_of(model, share):
    tile = ROWS * LANES
    return (
        (2 * model * share // tile, 2, False),
        (model * share // tile, 2, True),
        (2 * model * share // tile, 4, True),
    )


def kernel(
    users,
    seqs,
    raw_hbm,
    user_ref,
    place_ref,
    counts_ref,
    length_hbm,
    cot_hbm,
    enc_in_hbm,
    enc_out_hbm,
    proj_w_hbm,
    proj_b_ref,
    out_w_hbm,
    out_b_ref,
    layer_ref,
    full,
    bias_ref,
    send_buf,
    rows_sc,
    spot_out,
    spot_in,
    seq_sc,
    norm_sc,
    proj_sc,
    gate_sc,
    v_sc,
    k_sc,
    qb,
    gb,
    w_sc,
    s_sc,
    att,
    dq,
    dk,
    dv,
    d_mix,
    dproj,
    stat_out,
    stat_in,
    mix_own,
    mix_in,
    work,
    landing,
    bias,
    bias_in,
    raw_ref,
    cots,
    enc_in_ref,
    enc_out_ref,
    proj_w_ref,
    out_w_ref,
    a2a_send,
    a2a_recv,
    spot_send,
    spot_recv,
    x_send,
    x_recv,
    xs_send,
    xs_recv,
    n_send,
    n_recv,
    cot_sem,
    stat_sem,
    mix_sem,
    q_send,
    q_recv,
    g_send,
    g_recv,
    rs_send,
    rs_recv,
    ag_send,
    ag_recv,
    core_send,
    core_recv,
    b_send,
    b_recv,
    in_sem,
    length_sm,
    length_sem,
):
    me_u = lax.axis_index("users")
    me_s = lax.axis_index("seq")
    MESH = pl.DeviceIdType.MESH
    slots, model = raw_ref.shape
    block = layer_ref.shape[0]
    span = 2 * block
    width = out_w_ref.shape[0]
    share = width // 2
    pairs = share // LANES
    cap_pad = send_buf.shape[1]
    halves = seqs // 2
    scale = HEAD ** (-0.5)
    mine = me_s % 2
    half = me_s // 2
    partner = (me_u, flip(me_s, 1))

    def at_half(h):
        return (me_u, h * 2 + mine)

    def remote(source, target, send_sem, recv_sem, device):
        return pltpu.make_async_remote_copy(
            src_ref=source,
            dst_ref=target,
            send_sem=send_sem,
            recv_sem=recv_sem,
            device_id=device,
            device_id_type=MESH,
        )

    barrier = pltpu.get_barrier_semaphore()
    greeted = [(lax.rem(me_u + delta, users), me_s) for delta in range(1, users)]
    greeted += [partner]
    greeted += [at_half(lax.rem(half + delta, halves)) for delta in range(1, halves)]
    for device in greeted:
        pl.semaphore_signal(barrier, inc=1, device_id=device, device_id_type=MESH)

    def own_columns(part):
        return pl.ds(pl.multiple_of(part * width + mine * share, LANES), share)

    length_load = pltpu.make_async_copy(length_hbm, length_sm, length_sem)
    length_load.start()
    parts = (0, 2, 1, 3)
    loads = [
        pltpu.make_async_copy(source, target, in_sem.at[i])
        for i, (source, target) in enumerate(
            [
                (raw_hbm, raw_ref),
                (cot_hbm, cots.at[mine]),
                (out_w_hbm, out_w_ref),
                (enc_in_hbm, enc_in_ref),
                (enc_out_hbm, enc_out_ref),
            ]
            + [
                (
                    proj_w_hbm.at[:, own_columns(part)],
                    proj_w_ref.at[:, i * share : (i + 1) * share],
                )
                for i, part in enumerate(parts)
            ]
        )
    ]
    for load in loads:
        load.start()

    target = user_ref[...]
    lane_row = lax.broadcasted_iota(jnp.int32, (1, slots), 1)
    first = jnp.zeros((1, slots), jnp.int32)
    total = jnp.int32(0)
    for u in range(users):
        first = jnp.where(target == u, total, first)
        total = total + counts_ref[0, u]
    flat = jnp.where(lane_row < total, target * cap_pad + lane_row - first, -1)
    hot = lax.broadcasted_iota(jnp.int32, (users * cap_pad, slots), 0) == flat
    local_place = (place_ref[...] - me_s * block + 1).astype(F32)
    spots = jnp.sum(jnp.where(hot, local_place, 0.0), axis=1, keepdims=True) - 1.0
    diagonal = lax.broadcasted_iota(
        jnp.int32, (users, cap_pad, LANES), 1
    ) == lax.broadcasted_iota(jnp.int32, (users, cap_pad, LANES), 2)
    spot_out[...] = jnp.sum(
        jnp.where(diagonal, spots.reshape(users, cap_pad, 1), 0.0), axis=1, keepdims=True
    )
    loads[0].wait()
    bucket = dot(hot.astype(F32).astype(BF16), raw_ref[...]).astype(BF16)
    send_buf[...] = bucket.reshape(users, cap_pad, model)

    pl.semaphore_wait(barrier, len(greeted))

    order = list(range(1, users))

    def spot_copy(d):
        peer = flip_all(me_u, d)
        return remote(
            spot_out.at[peer], spot_in.at[half, me_u], spot_send.at[d], spot_recv.at[d], (peer, me_s)
        )

    def row_copy(d):
        peer = flip_all(me_u, d)
        return remote(
            send_buf.at[peer], rows_sc.at[half, me_u], a2a_send.at[d], a2a_recv.at[d], (peer, me_s)
        )

    def relay(h, d, delta):
        source = flip_all(me_u, d)
        held = send_buf.at[source] if d == 0 else rows_sc.at[h, source]
        return remote(
            held,
            rows_sc.at[h, source],
            x_send.at[delta - 1, d],
            x_recv.at[delta - 1, d],
            at_half(h + delta),
        )

    def relay_spots(h, delta):
        return remote(
            spot_in.at[h],
            spot_in.at[h],
            xs_send.at[delta - 1],
            xs_recv.at[delta - 1],
            at_half(h + delta),
        )

    def above(delta):
        return half + delta < halves

    def below(delta):
        return half >= delta

    for d in order:
        spot_copy(d).start()
    for d in order:
        row_copy(d).start()
    for delta in range(1, halves):

        @pl.when(above(delta))
        def _():
            relay(half, 0, delta).start()

    loads[1].wait()
    cot_copy = remote(cots.at[mine], cots.at[mine], cot_sem.at[0], cot_sem.at[1], partner)
    cot_copy.start()
    rows_sc[half, me_u] = send_buf[me_u]
    spot_in[half, me_u] = spot_out[me_u]

    length_load.wait()
    length = length_sm[0]
    rows = lax.broadcasted_iota(jnp.int32, (block, 1), 0)

    def block_rows(index):
        return pl.ds(pl.multiple_of(index * block, block), block)

    own_rows, other_rows = block_rows(mine), block_rows(1 - mine)

    def present_at(index):
        return (half * 2 + index) * block + rows < length

    out_rows = pl.ds(pl.multiple_of(mine * share, LANES), share)
    out_rows_other = pl.ds(pl.multiple_of((1 - mine) * share, LANES), share)
    loads[2].wait()

    def mask_cot(index):
        d_out = jnp.where(
            present_at(index), cots[index], jnp.zeros((block, model), BF16)
        )
        d_mix[block_rows(index), :] = dot(d_out, out_w_ref[out_rows, :], (1, 1))

    mask_cot(mine)
    for load in loads[3:]:
        load.wait()
    bias_row = jnp.concatenate([proj_b_ref[:, own_columns(part)] for part in parts], axis=1)
    att[...] = jnp.zeros_like(att)
    dq[...] = jnp.zeros_like(dq)
    dk[...] = jnp.zeros_like(dk)
    dv[...] = jnp.zeros_like(dv)
    cot_copy.wait_recv()
    mask_cot(1 - mine)

    for d in order:
        row_copy(d).wait_recv()
        for delta in range(1, halves):

            @pl.when(above(delta))
            def _():
                relay(half, d, delta).start()

    for d in order:
        spot_copy(d).wait_recv()
    for delta in range(1, halves):

        @pl.when(above(delta))
        def _():
            relay_spots(half, delta).start()

    def ingest(h):
        arrived = rows_sc[h].reshape(users * cap_pad, model)
        where_to = jnp.sum(jnp.where(diagonal, spot_in[h], 0.0), axis=2, keepdims=True)
        where_to = where_to.reshape(users * cap_pad, 1).astype(jnp.int32)
        placed = (
            lax.broadcasted_iota(jnp.int32, (users * cap_pad, block), 1) == where_to
        ).astype(F32).astype(BF16)
        events = dot(placed, arrived, (0, 0)).astype(BF16)
        hidden = silu(dot(events, enc_in_ref[...])).astype(BF16)
        sequence = dot(hidden, enc_out_ref[...]).astype(BF16)
        norm_sc[h, mine] = layer_norm(sequence.astype(F32))[0].astype(BF16)
        return sequence

    def norm_copy(h):
        own = norm_sc.at[h, mine]
        return remote(own, own, n_send.at[h], n_recv.at[h], partner)

    seq_sc[...] = ingest(half)
    norm_copy(half).start()

    def project(index):
        at = block_rows(index)
        projected = dot(norm_sc[half, index], proj_w_ref[...]) + bias_row
        proj_sc[at, :] = projected
        gates = silu(projected).astype(BF16)
        gate_sc[at, :] = gates[:, :share]
        qb[half, at, :] = gates[:, share : 2 * share]
        v_sc[half, at, :] = gates[:, 2 * share : 3 * share]
        k_sc[half, at, :] = gates[:, 3 * share :]

    def project_low(h, index):
        at = block_rows(index)
        gates = silu(
            dot(norm_sc[h, index], proj_w_ref[:, 2 * share :]) + bias_row[:, 2 * share :]
        ).astype(BF16)
        v_sc[h, at, :] = gates[:, :share]
        k_sc[h, at, :] = gates[:, share:]

    def half_of(values, hh):
        zero = jnp.zeros_like(values)
        low = lax.broadcasted_iota(jnp.int32, values.shape, 1) < HEAD
        return jnp.where(low, values, zero) if hh == 0 else jnp.where(low, zero, values)

    def lanes(p):
        return slice(p * LANES, (p + 1) * LANES)

    def merge(low, high):
        keep = lax.broadcasted_iota(jnp.int32, low.shape, 1) < HEAD
        return jnp.where(keep, low, high)

    def scores_of(slot, q_half, qi, k_half, ki):
        qr, kr = block_rows(qi), block_rows(ki)
        bound = jnp.minimum((q_half * 2 + qi) * block + rows, length - 1)
        bound = bound - (k_half * 2 + ki) * block
        allowed = lax.broadcasted_iota(jnp.int32, (block, block), 1) <= bound
        for p in range(pairs):
            queries = qb[q_half, qr, lanes(p)]
            keys = k_sc[k_half, kr, lanes(p)]
            for hh in range(2):
                score = dot(half_of(queries, hh), keys, (1, 1)) * scale
                gate = sigmoid(score)
                plain = score * gate
                w_sc[slot, 2 * p + hh, qr, kr] = jnp.where(allowed, plain, 0.0).astype(BF16)
                s_sc[slot, 2 * p + hh, qr, kr] = jnp.where(
                    allowed, gate + plain * (1.0 - gate), 0.0
                )

    def attend(slot, qi, k_half, ki):
        qr, kr = block_rows(qi), block_rows(ki)
        for p in range(pairs):
            values = v_sc[k_half, kr, lanes(p)]
            att[qr, lanes(p)] = att[qr, lanes(p)] + merge(
                dot(w_sc[slot, 2 * p, qr, kr], values), dot(w_sc[slot, 2 * p + 1, qr, kr], values)
            )

    project(mine)

    def own_block(qi, ki):
        scores_of(half, half, qi, half, ki)
        attend(half, qi, half, ki)

    own_block(mine, mine)

    norm_copy(half).wait_recv()
    project(1 - mine)

    def q_copy(delta):
        return remote(
            qb.at[half], qb.at[half], q_send.at[delta - 1], q_recv.at[delta - 1], at_half(half - delta)
        )

    for delta in range(1, halves):

        @pl.when(below(delta))
        def _():
            q_copy(delta).start()

    own_block(1 - mine, 1 - mine)
    own_block(1, 0)

    for delta in range(1, halves):

        @pl.when(below(delta))
        def _():
            h = half - delta
            relay_spots(h, delta).wait_recv()
            for d in [0] + order:
                relay(h, d, delta).wait_recv()

    for delta in range(1, halves):

        @pl.when(below(delta))
        def _():
            h = half - delta
            ingest(h)
            norm_copy(h).start()
            for ki in (mine, 1 - mine):
                if ki is not mine:
                    norm_copy(h).wait_recv()
                project_low(h, ki)
                for qi in range(2):
                    scores_of(h, half, qi, h, ki)
                    attend(h, qi, h, ki)

    attended = att[...]
    gate_u = gate_sc[...].astype(F32)
    d_mixed = d_mix[...]
    d_onorm = d_mixed * gate_u
    own_mean = jnp.mean(attended, axis=-1, keepdims=True)
    center = attended - own_mean
    facts = (
        own_mean,
        jnp.sum(center * center, axis=-1, keepdims=True),
        jnp.sum(d_onorm, axis=-1, keepdims=True),
        jnp.sum(d_onorm * center, axis=-1, keepdims=True),
    )
    tall = span // LANES
    square = lax.broadcasted_iota(jnp.int32, (tall, LANES, LANES), 1) == lax.broadcasted_iota(
        jnp.int32, (tall, LANES, LANES), 2
    )
    for i, fact in enumerate(facts):
        stat_out[i] = jnp.sum(
            jnp.where(square, fact.reshape(tall, LANES, 1), 0.0), axis=1, keepdims=True
        )
    stat_copy = remote(stat_out, stat_in, stat_sem.at[0], stat_sem.at[1], partner)
    stat_copy.start()

    stat_copy.wait_recv()
    theirs = [
        jnp.sum(jnp.where(square, stat_in[i], 0.0), axis=2, keepdims=True).reshape(span, 1)
        for i in range(len(facts))
    ]
    mean = 0.5 * (own_mean + theirs[0])
    gap = own_mean - theirs[0]
    variance = (facts[1] + theirs[1] + gap * gap * (0.5 * share)) / width
    inverse = lax.rsqrt(variance + EPSILON)
    mean_d = (facts[2] + theirs[2]) / width
    mean_do = (
        (facts[3] + theirs[3] + (own_mean - mean) * facts[2] + (theirs[0] - mean) * theirs[2])
        * inverse
        / width
    )
    onorm = (attended - mean) * inverse
    d_att = ((d_onorm - mean_d - onorm * mean_do) * inverse).astype(BF16)
    gb[half] = d_att

    def g_copy(delta, qi):
        piece = gb.at[half, qi * block : (qi + 1) * block]
        return remote(
            piece, piece, g_send.at[delta - 1, qi], g_recv.at[delta - 1, qi], at_half(half - delta)
        )

    for delta in range(1, halves):

        @pl.when(below(delta))
        def _():
            for qi in range(2):
                g_copy(delta, qi).start()

    mixed = (onorm * gate_u).astype(BF16)
    mix_own[...] = mixed
    mix_copy = remote(mix_own.at[other_rows], mix_in, mix_sem.at[0], mix_sem.at[1], partner)
    mix_copy.start()
    dproj[:, :share] = (d_mixed * onorm * silu_grad(proj_sc[:, :share])).astype(BF16)
    positions = lax.broadcasted_iota(jnp.int32, (span, 1), 0)
    present = half * span + positions < length
    d_out = jnp.where(present, cots[...].reshape(span, model), jnp.zeros((span, model), BF16))
    normed = norm_sc[half].reshape(span, model)
    column = jnp.sum(d_out.astype(F32), axis=0, keepdims=True)
    bias[0] = jnp.zeros_like(bias[0])
    bias[0, 1:2, : model // 2] = jnp.where(
        mine == 0, column[:, : model // 2], column[:, model // 2 :]
    )
    (early, middle, late), stages, total_chunks = plan_of(users, seqs, groups_of(model, share))
    middle_base, late_base = middle[0][0], late[0][0]

    def store_tiles(base, values):
        height = values.shape[0] // ROWS
        for tile in range(values.shape[1] // LANES):
            work[base + tile * height : base + (tile + 1) * height] = values[
                :, tile * LANES : (tile + 1) * LANES
            ].reshape(height, ROWS, LANES)
        return base + values.shape[0] * values.shape[1] // (ROWS * LANES)

    def clear(base, stop):
        if base < stop:
            work[base:stop] = jnp.zeros((stop - base, ROWS, LANES), BF16)

    filled = store_tiles(0, dot(mixed, d_out, (0, 0)).astype(BF16))
    filled = store_tiles(filled, dot(normed, dproj[:, :share], (0, 0)).astype(BF16))
    clear(filled, middle_base)

    def place_of(axis, bit):
        own = me_s if axis == "seq" else me_u
        peer = flip(own, bit)
        device = (me_u, peer) if axis == "seq" else (peer, me_s)
        return (own // bit) % 2, device

    all_streams = early + middle + late
    starts = []
    for base, size, bit_order in all_streams:
        offsets = [base]
        for stage in range(stages):
            side, _ = place_of(*bit_order[stage])
            offsets.append(offsets[stage] + side * (size >> (stage + 1)))
        starts.append(offsets)
    landings = []
    landing_at = 0
    for base, size, _ in all_streams:
        offsets = []
        for stage in range(stages):
            offsets.append(landing_at)
            landing_at += size >> (stage + 1)
        landings.append(offsets)
    early_ids = list(range(len(early)))
    middle_ids = list(range(len(early), len(early) + len(middle)))
    late_ids = list(range(len(early) + len(middle), len(all_streams)))

    def reduce_copy(i, stage):
        base, size, bit_order = all_streams[i]
        side, device = place_of(*bit_order[stage])
        part = size >> (stage + 1)
        start = starts[i][stage]
        return (
            remote(
                work.at[pl.ds(start + (1 - side) * part, part)],
                landing.at[pl.ds(landings[i][stage], part)],
                rs_send.at[i, stage],
                rs_recv.at[i, stage],
                device,
            ),
            start + side * part,
            part,
        )

    def quad_of(i, mask):
        base, size, bit_order = all_streams[i]
        (axis_a, bit_a), (axis_b, bit_b) = bit_order[stages - 2 :]
        place = {"users": me_u, "seq": me_s}
        side_a, side_b = (place[axis_a] // bit_a) % 2, (place[axis_b] // bit_b) % 2
        if mask & 2:
            place[axis_a] = flip(place[axis_a], bit_a)
            side_a = 1 - side_a
        if mask & 1:
            place[axis_b] = flip(place[axis_b], bit_b)
            side_b = 1 - side_b
        part = size >> stages
        theirs = starts[i][stages - 2] + (2 * side_a + side_b) * part
        return (place["users"], place["seq"]), theirs, part

    def reduce_quad_copy(i, mask):
        device, theirs, part = quad_of(i, mask)
        slot = stages - 3 + mask
        return remote(
            work.at[pl.ds(theirs, part)],
            landing.at[pl.ds(landings[i][stages - 2] + (mask - 1) * part, part)],
            rs_send.at[i, slot],
            rs_recv.at[i, slot],
            device,
        )

    def gather_quad_copy(i, mask):
        device, _, part = quad_of(i, mask)
        slot = stages - 3 + mask
        own = full.at[mine, pl.ds(starts[i][stages], part)]
        return remote(own, own, ag_send.at[i, slot], ag_recv.at[i, slot], device)

    def reduce_quad(ids):
        for i in ids:
            part = all_streams[i][1] >> stages
            own = pl.ds(starts[i][stages], part)
            summed = work[own].astype(F32)
            for mask in QUAD:
                reduce_quad_copy(i, mask).wait()
                at = landings[i][stages - 2] + (mask - 1) * part
                summed = summed + landing[at : at + part].astype(F32)
            full[mine, own] = summed.astype(BF16)
            for mask in QUAD:
                gather_quad_copy(i, mask).start()

    def gather_quad(ids):
        for i in ids:
            for mask in QUAD:
                gather_quad_copy(i, mask).wait()
            gather_copy(i, stages - 3).start()
            if stages == 3:
                core_copy(i, 0).start()

    def gather_copy(i, stage):
        base, size, bit_order = all_streams[i]
        _, device = place_of(*bit_order[stage])
        own = full.at[mine, pl.ds(starts[i][stage + 1], size >> (stage + 1))]
        return remote(own, own, ag_send.at[i, stage], ag_recv.at[i, stage], device)

    def core_copy(i, second):
        base, size, bit_order = all_streams[i]
        side, _ = place_of(*bit_order[0])
        part = size >> 1
        start = base + (1 - side) * part if second else base + side * part
        own = full.at[mine, pl.ds(start, part)]
        return remote(own, own, core_send.at[i, second], core_recv.at[i, second], partner)

    def reduce_start(ids):
        for i in ids:
            reduce_copy(i, 0)[0].start()

    def reduce_step(ids, stage):
        for i in ids:
            copy, keep, part = reduce_copy(i, stage)
            copy.wait()
            at = landings[i][stage]
            summed = (
                work[pl.ds(keep, part)].astype(F32) + landing[at : at + part].astype(F32)
            ).astype(BF16)
            work[pl.ds(keep, part)] = summed
            if stage + 1 < stages - 2:
                reduce_copy(i, stage + 1)[0].start()
            else:
                for mask in QUAD:
                    reduce_quad_copy(i, mask).start()

    def gather_step(ids, stage):
        for i in ids:
            gather_copy(i, stage).wait()
            if stage > 0:
                gather_copy(i, stage - 1).start()
                if stage == 1:
                    core_copy(i, 0).start()
            else:
                core_copy(i, 1).start()

    def core_finish(ids):
        for i in ids:
            core_copy(i, 0).wait()
            core_copy(i, 1).wait()

    def advance(ids, turn):
        if turn < stages - 2:
            reduce_step(ids, turn)
        elif turn == stages - 2:
            reduce_quad(ids)
        elif turn == stages - 1:
            gather_quad(ids)
        elif turn < 2 * stages - 2:
            gather_step(ids, 2 * stages - 3 - turn)
        elif turn == 2 * stages - 2:
            core_finish(ids)

    reduce_start(early_ids)

    for delta in range(1, halves):

        @pl.when(above(delta))
        def _():
            h = half + delta
            remote(
                qb.at[h], qb.at[h], q_send.at[delta - 1], q_recv.at[delta - 1], at_half(half)
            ).wait_recv()
            for qi in range(2):
                for ki in range(2):
                    scores_of(h, h, qi, half, ki)

    def backward(slot, q_half, k_half, qi, keys_to, query_side, key_side):
        qr = slice(qi * block, (qi + 1) * block)
        kr = slice(0, keys_to * block)
        for p in range(pairs):
            at = lanes(p)
            grads = gb[q_half, qr, at]
            values = v_sc[k_half, kr, at]
            d_scores = []
            for hh in range(2):
                d_weight = dot(half_of(grads, hh), values, (1, 1))
                d_scores.append((d_weight * s_sc[slot, 2 * p + hh, qr, kr]).astype(BF16))
            if query_side:
                keys = k_sc[k_half, kr, at]
                dq[qr, at] = dq[qr, at] + merge(dot(d_scores[0], keys), dot(d_scores[1], keys))
            if key_side:
                queries = qb[q_half, qr, at]
                dk[kr, at] = dk[kr, at] + merge(
                    dot(d_scores[0], queries, (0, 0)), dot(d_scores[1], queries, (0, 0))
                )
                dv[kr, at] = dv[kr, at] + merge(
                    dot(w_sc[slot, 2 * p, qr, kr], grads, (0, 0)),
                    dot(w_sc[slot, 2 * p + 1, qr, kr], grads, (0, 0)),
                )

    for qi in range(2):
        backward(half, half, half, qi, qi + 1, True, True)

    for delta in range(1, halves):

        @pl.when(below(delta))
        def _():
            h = half - delta
            for qi in range(2):
                backward(h, half, h, qi, 2, True, False)

    def finish_part(index, buf, factor):
        at = slice(index * share, (index + 1) * share)
        dproj[:, at] = (buf[...] * factor * silu_grad(proj_sc[:, at])).astype(BF16)

    finish_part(1, dq, scale)
    filled = store_tiles(
        middle_base, dot(normed, dproj[:, share : 2 * share], (0, 0)).astype(BF16)
    )
    clear(filled, late_base)
    reduce_start(middle_ids)

    advance(early_ids, 0)

    for delta in range(1, halves):

        @pl.when(above(delta))
        def _():
            h = half + delta
            for qi in range(2):
                piece = gb.at[h, qi * block : (qi + 1) * block]
                remote(
                    piece, piece, g_send.at[delta - 1, qi], g_recv.at[delta - 1, qi], at_half(half)
                ).wait_recv()
                backward(h, h, half, qi, 2, False, True)

    finish_part(2, dv, 1.0)
    finish_part(3, dk, scale)
    filled = store_tiles(late_base, dot(normed, dproj[:, 2 * share :], (0, 0)).astype(BF16))
    clear(filled, total_chunks)
    reduce_start(late_ids)
    bias[0, 0:1, :] = jnp.sum(dproj[...].astype(F32), axis=0, keepdims=True)

    def bias_copy(stage):
        _, device = place_of(*all_streams[late_ids[0]][2][stage])
        return remote(
            bias.at[stage], bias_in.at[stage], b_send.at[stage], b_recv.at[stage], device
        )

    def bias_step(stage):
        bias_copy(stage).wait()
        bias[stage + 1] = bias[stage] + bias_in[stage]
        if stage + 1 < stages:
            bias_copy(stage + 1).start()

    bias_copy(0).start()

    mix_copy.wait_recv()
    result = (
        dot(mix_own[own_rows, :], out_w_ref[out_rows, :])
        + dot(mix_in[...], out_w_ref[out_rows_other, :])
        + out_b_ref[...]
        + seq_sc[...].astype(F32)
    )
    layer_ref[...] = jnp.where(present_at(mine), result, 0.0).astype(BF16)

    for turn in range(2 * stages - 1):
        advance(late_ids, turn)
        if turn < stages:
            bias_step(turn)
        if turn == stages:
            bias_ref[mine] = bias[stages]
            bias_own = bias_ref.at[mine]
            bias_final = remote(bias_own, bias_own, b_send.at[stages], b_recv.at[stages], partner)
            bias_final.start()
        advance(middle_ids, turn)
        advance(early_ids, turn + 1)

    bias_final.wait()
    for d in order:
        spot_copy(d).wait_send()
        row_copy(d).wait_send()
    cot_copy.wait_send()
    stat_copy.wait_send()
    mix_copy.wait_send()
    norm_copy(half).wait_send()
    for delta in range(1, halves):

        @pl.when(above(delta))
        def _():
            relay_spots(half, delta).wait_send()
            for d in [0] + order:
                relay(half, d, delta).wait_send()

        @pl.when(below(delta))
        def _():
            norm_copy(half - delta).wait_send()
            q_copy(delta).wait_send()
            for qi in range(2):
                g_copy(delta, qi).wait_send()


def unpack(full, bias_ref, layer_in, layer_ref, gpw_ref, gpb_ref, gow_ref, gob_ref, bases):
    model, width = gow_ref.shape[1], gow_ref.shape[0]
    share = width // 2
    layer_ref[...] = layer_in[...]

    for plane in range(2):
        for i, part in enumerate((0, 2, 1, 3)):
            low = part * width + plane * share
            gpb_ref[:, low : low + share] = bias_ref[plane, 0:1, i * share : (i + 1) * share]
        low = plane * (model // 2)
        gob_ref[:, low : low + model // 2] = bias_ref[plane, 1:2, : model // 2]

        def tile_of(base, height):
            return full[plane, base : base + height // ROWS].reshape(height, LANES)

        at = 0
        rows = slice(plane * share, (plane + 1) * share)
        for tile in range(model // LANES):
            gow_ref[rows, tile * LANES : (tile + 1) * LANES] = tile_of(at, share)
            at += share // ROWS
        size = model // ROWS
        per = share // LANES
        spots = (
            (0, at),
            (2, bases[1]),
            (1, bases[2]),
            (3, bases[2] + per * size),
        )
        for part, at in spots:
            for tile in range(per):
                low = part * width + plane * share + tile * LANES
                gpw_ref[:, low : low + LANES] = tile_of(at + tile * size, model)


def on_device(
    users,
    seqs,
    raw_events,
    target_user,
    target_place,
    send_counts,
    lengths,
    cotangent,
    encoder_in,
    encoder_out,
    proj_weight,
    proj_bias,
    out_weight,
    out_bias,
):
    slots = raw_events.shape[1]
    block, model = cotangent.shape[1], cotangent.shape[2]
    width = out_weight.shape[0]
    share = width // 2
    span = 2 * block
    halves = seqs // 2
    heads = share // HEAD
    others = max(halves - 1, 1)
    cap_pad = -(-(slots // users) // ROWS) * ROWS
    plans, stages, total = plan_of(users, seqs, groups_of(model, share))
    count = sum(len(plan) for plan in plans)
    vmem = pl.BlockSpec(memory_space=pltpu.VMEM)
    anywhere = pl.BlockSpec(memory_space=pl.ANY)
    smem = pl.BlockSpec(memory_space=pltpu.SMEM)
    dma = pltpu.SemaphoreType.DMA
    resident = 2 * total <= RESIDENT
    result = pltpu.VMEM if resident else jax.ShapeDtypeStruct
    layer, full, bias = pl.pallas_call(
        functools.partial(kernel, users, seqs),
        out_shape=(
            result((block, model), BF16),
            result((2, total, ROWS, LANES), BF16),
            result((2, 2, 4 * share), F32),
        ),
        in_specs=[anywhere, vmem, vmem, smem, pl.BlockSpec(memory_space=pltpu.HBM)]
        + [anywhere] * 4 + [vmem, anywhere, vmem],
        out_specs=(vmem,) * 3,
        scratch_shapes=[
            pltpu.VMEM((users, cap_pad, model), BF16),
            pltpu.VMEM((halves, users, cap_pad, model), BF16),
            pltpu.VMEM((users, 1, LANES), F32),
            pltpu.VMEM((halves, users, 1, LANES), F32),
            pltpu.VMEM((block, model), BF16),
            pltpu.VMEM((halves, 2, block, model), BF16),
            pltpu.VMEM((span, 4 * share), F32),
            pltpu.VMEM((span, share), BF16),
            pltpu.VMEM((halves, span, share), BF16),
            pltpu.VMEM((halves, span, share), BF16),
            pltpu.VMEM((halves, span, share), BF16),
            pltpu.VMEM((halves, span, share), BF16),
            pltpu.VMEM((halves, heads, span, span), BF16),
            pltpu.VMEM((halves, heads, span, span), F32),
            pltpu.VMEM((span, share), F32),
            pltpu.VMEM((span, share), F32),
            pltpu.VMEM((span, share), F32),
            pltpu.VMEM((span, share), F32),
            pltpu.VMEM((span, share), F32),
            pltpu.VMEM((span, 4 * share), BF16),
            pltpu.VMEM((4, span // LANES, 1, LANES), F32),
            pltpu.VMEM((4, span // LANES, 1, LANES), F32),
            pltpu.VMEM((span, share), BF16),
            pltpu.VMEM((block, share), BF16),
            pltpu.VMEM((total, ROWS, LANES), BF16),
            pltpu.VMEM((total, ROWS, LANES), BF16),
            pltpu.VMEM((stages + 1, 2, 4 * share), F32),
            pltpu.VMEM((stages, 2, 4 * share), F32),
            pltpu.VMEM(raw_events.shape[1:], BF16),
            pltpu.VMEM((2, block, model), BF16),
            pltpu.VMEM(encoder_in.shape, BF16),
            pltpu.VMEM(encoder_out.shape, BF16),
            pltpu.VMEM((model, 4 * share), BF16),
            pltpu.VMEM(out_weight.shape, BF16),
            dma((users,)),
            dma((users,)),
            dma((users,)),
            dma((users,)),
            dma((others, users)),
            dma((others, users)),
            dma((others,)),
            dma((others,)),
            dma((halves,)),
            dma((halves,)),
            dma((2,)),
            dma((2,)),
            dma((2,)),
            dma((others,)),
            dma((others,)),
            dma((others, 2)),
            dma((others, 2)),
            dma((count, stages + 1)),
            dma((count, stages + 1)),
            dma((count, stages + 1)),
            dma((count, stages + 1)),
            dma((count, 2)),
            dma((count, 2)),
            dma((stages + 1,)),
            dma((stages + 1,)),
            dma((9,)),
            pltpu.SMEM(lengths.shape, jnp.int32),
            dma,
        ],
        compiler_params=pltpu.CompilerParams(
            collective_id=0, has_side_effects=True, vmem_limit_bytes=60000 * 1024
        ),
    )(
        raw_events[0],
        target_user,
        target_place,
        send_counts[0],
        lengths,
        cotangent[0],
        encoder_in,
        encoder_out,
        proj_weight,
        proj_bias[None],
        out_weight,
        out_bias[None],
    )
    held = (full, bias, layer)
    if resident:
        held = [pltpu.with_memory_space_constraint(array, pltpu.VMEM) for array in held]
    layer_out, grad_pw, grad_pb, grad_ow, grad_ob = pl.pallas_call(
        functools.partial(unpack, bases=[plan[0][0] for plan in plans]),
        out_shape=(
            jax.ShapeDtypeStruct((block, model), BF16),
            jax.ShapeDtypeStruct((model, 4 * width), BF16),
            jax.ShapeDtypeStruct((1, 4 * width), F32),
            jax.ShapeDtypeStruct((width, model), BF16),
            jax.ShapeDtypeStruct((1, model), F32),
        ),
        in_specs=[vmem] * 3,
        out_specs=(vmem,) * 5,
    )(*held)
    return layer_out[None], grad_pw, grad_pb[0], grad_ow, grad_ob[0]


def solution(mesh):
    placed = (
        P("seq", "users", None),
        P("seq", "users"),
        P("seq", "users"),
        P("seq", "users", None),
        P("users"),
        P("users", "seq", None),
        P(),
        P(),
        P(),
        P(),
        P(),
        P(),
    )
    return jax.shard_map(
        functools.partial(on_device, mesh.shape["users"], mesh.shape["seq"]),
        mesh=mesh,
        in_specs=placed,
        out_specs=(P("users", "seq", None), P(), P(), P(), P()),
        check_vma=False,
    )
```
